512 devices in a mesh: tm: 8 (over x, core), tile: 64 (over y, z).
Axes of the slice: x: 4, y: 4, z: 16, core: 2. Of those that a mesh axis runs over, the one named last changes fastest.
Arguments:
- starts: float32 [8, 98304, 128], P('tm', 'tile'), may hold values from -6 to 6
- sources: float32 [98304, 128], P('tile'), may hold values from -6 to 6
- fine_ops: float32 [8, 768, 4, 128, 128], P('tm', 'tile'), may hold values from -0.1875 to 0.1875
- col_index: int32 [8, 768, 4], P('tm', 'tile'), may hold values from 0 to 15, as said below
- live_count: int32 [8, 768], P('tm', 'tile'), may hold values from 1 to 4, as said below
- coarse_op: float32 [24576, 768], P('tile'), may hold values from -0.15625 to 0.15625
- cell_map: int32 [98304], P('tile'), may hold values from 0 to 383, as said below
Outputs:
- corrected: float32 [8, 98304, 128], P('tm', 'tile')
The draws below stay inside these ranges and needn't reach their ends.
Inputs may be any that keep to these rules, and one draw needn't show every extreme that they name: `col_index`: each entry names one of the 16 blocks of a tile's fine window. Slots from live_count on are padding and carry no transport. `cell_map`: each entry is a local coarse index within its own tile; every coarse cell of every tile has at least one fine cell.
All inputs are finite; a program needn't handle non-finite values.
Results may differ from the reference program's by a relative error of at most 0.0003.
Values sent between devices are 32-bit elements; how exact they have to be, the bound alone decides.
No kernel may reach another device: no remote copies, remote signals or barrier semaphores. Data moves between devices by JAX's collectives and lax.ppermute only.
A program may use at most 64 MiB of HBM per device.

```python
import jax
import jax.numpy as jnp
from jax import lax

NTR = 128
BS = 128
ROWS = 1536
HALO = 256
KMAX = 4
STEPS = 2
SLICES = 8
CELLS = 98304
COARSE = 384
CHALO = 192


def draw_col_index(key, part):
    tile_count = CELLS // ROWS
    block_count = ROWS // BS
    window = (ROWS + 2 * HALO) // BS
    key_cols = jax.random.fold_in(key, 11)
    key_pick = jax.random.fold_in(key, 12)
    columns = jax.random.randint(key_cols, (SLICES, tile_count, block_count, KMAX), 0, window)
    chosen = jax.random.randint(key_pick, (SLICES, tile_count, 1, 1), 0, block_count)
    block_ids = jnp.arange(block_count)[None, None, :, None]
    slot_ids = jnp.arange(KMAX)[None, None, None, :]
    columns = jnp.where((block_ids == chosen) & (slot_ids == 0), window - 1, columns)
    columns = jnp.where((block_ids == chosen) & (slot_ids == 1), 0, columns)
    return columns.reshape(SLICES, CELLS // BS, KMAX).astype(jnp.int32)


def draw_live_count(key, part):
    tile_count = CELLS // ROWS
    block_count = ROWS // BS
    key_cap = jax.random.fold_in(key, 21)
    key_top = jax.random.fold_in(key, 22)
    key_fill = jax.random.fold_in(key, 23)
    key_pick = jax.random.fold_in(key, 24)
    key_low = jax.random.fold_in(key, 25)
    ceilings = jax.random.randint(key_cap, (SLICES, tile_count), 2, KMAX + 1)
    busiest = jax.random.randint(key_top, (SLICES, 1), 0, tile_count)
    ceilings = jnp.where(jnp.arange(tile_count)[None, :] == busiest, KMAX, ceilings)
    counted = jax.random.randint(key_fill, (SLICES, tile_count, block_count), 1, ceilings[:, :, None] + 1)
    chosen = jax.random.randint(key_pick, (SLICES, tile_count, 1), 0, block_count)
    lowest = (chosen + 1 + jax.random.randint(key_low, (SLICES, tile_count, 1), 0, block_count - 1)) % block_count
    block_ids = jnp.arange(block_count)[None, None, :]
    counted = jnp.where(block_ids == chosen, ceilings[:, :, None], counted)
    counted = jnp.where(block_ids == lowest, 1, counted)
    return counted.reshape(SLICES, CELLS // BS).astype(jnp.int32)


def draw_cell_map(key, part):
    tile_count = CELLS // ROWS
    key_map = jax.random.fold_in(key, 31)
    key_perm = jax.random.fold_in(key, 32)
    mapping = jax.random.randint(key_map, (tile_count, ROWS), 0, COARSE)
    orders = jax.vmap(lambda sub_key: jax.random.permutation(sub_key, ROWS))(jax.random.split(key_perm, tile_count))
    mapping = mapping.at[jnp.arange(tile_count)[:, None], orders[:, :COARSE]].set(jnp.arange(COARSE, dtype=jnp.int32)[None, :])
    return mapping.reshape(CELLS).astype(jnp.int32)


def shard_levels(stream_key, extent, cuts, smallest, top_value):
    level, own = 1.0, jax.random.fold_in(stream_key, 6)
    for position, shards_of in cuts:
        heights = jnp.exp(jax.random.uniform(jax.random.fold_in(own, position), (shards_of,), jnp.float32, smallest / len(cuts), top_value / len(cuts)))
        level = level * jnp.repeat(heights, extent[position] // shards_of).reshape([-1 if axis == position else 1 for axis in range(len(extent))])
    return level


def centred(stream_key, extent, scale, limit, cuts=(), held_as=jnp.bfloat16):
    values = scale * jax.random.normal(stream_key, extent, jnp.float32)
    if cuts:
        values = values * shard_levels(stream_key, extent, cuts, -0.22, 0.18)
    return jnp.clip(values, -limit, limit).astype(held_as)


def setup_inputs(seed: int = 0) -> dict:
    arg_keys = jax.random.split(jax.random.key(seed), 8)
    return {
        "starts": centred(arg_keys[0], (SLICES, CELLS, NTR), 1.0, 6.0, ((0, 8), (1, 64)), jnp.float32),
        "sources": centred(arg_keys[1], (CELLS, NTR), 1.0, 6.0, ((0, 64),), jnp.float32),
        "fine_ops": centred(arg_keys[2], (SLICES, CELLS // BS, KMAX, BS, BS), (2 * KMAX * BS) ** -0.5, 0.1875, ((0, 8), (1, 64)), jnp.float32),
        "col_index": draw_col_index(jax.random.fold_in(arg_keys[7], 71), 0),
        "live_count": draw_live_count(jax.random.fold_in(arg_keys[7], 71), 0),
        "coarse_op": centred(arg_keys[5], (CELLS // 4, COARSE + 2 * CHALO), (2 * (COARSE + 2 * CHALO)) ** -0.5, 0.15625, ((0, 64),), jnp.float32),
        "cell_map": draw_cell_map(jax.random.fold_in(arg_keys[7], 71), 0),
    }


def extend(tiled, width):
    lower_rim = jnp.roll(tiled, 1, axis=0)[:, tiled.shape[1] - width:]
    upper_rim = jnp.roll(tiled, -1, axis=0)[:, :width]
    return jnp.concatenate([lower_rim, tiled, upper_rim], axis=1)


def fine_step(tracer_state, sources, transport, columns, slot_counts):
    tile_count = CELLS // ROWS
    block_count = ROWS // BS
    extended = extend(tracer_state.reshape(tile_count, ROWS, NTR), HALO)
    extended = extended.reshape(tile_count, (ROWS + 2 * HALO) // BS, BS, NTR)

    def one_tile(packed):
        ext_blocks, block_ops, block_cols, block_counts = packed
        live_mask = (jnp.arange(KMAX)[None, :] < block_counts[:, None]).astype(jnp.float32)
        pieces = ext_blocks[block_cols] * live_mask[:, :, None, None]
        return jnp.einsum("bkij,bkjn->bin", block_ops, pieces, precision=lax.Precision.HIGHEST)

    transported = lax.map(one_tile, (extended,
                                     transport.reshape(tile_count, block_count, KMAX, BS, BS),
                                     columns.reshape(tile_count, block_count, KMAX),
                                     slot_counts.reshape(tile_count, block_count)))
    return transported.reshape(CELLS, NTR) + sources


def coarse_apply(coarse_state, coarse_op):
    tile_count = CELLS // ROWS
    extended = extend(coarse_state.reshape(tile_count, COARSE, NTR), CHALO)
    operator = coarse_op.reshape(tile_count, COARSE, COARSE + 2 * CHALO)
    result = jnp.einsum("tcj,tjn->tcn", operator, extended, precision=lax.Precision.HIGHEST)
    return result.reshape(tile_count * COARSE, NTR)


def reference(starts, sources, fine_ops, col_index, live_count, coarse_op, cell_map):
    tile_count = CELLS // ROWS
    tiled_map = cell_map.reshape(tile_count, ROWS)
    onehot = (tiled_map[:, :, None] == jnp.arange(COARSE, dtype=jnp.int32)[None, None, :]).astype(jnp.float32)
    children = jnp.sum(onehot, axis=1)

    def restrict(values_in):
        sums = jnp.einsum("tic,tin->tcn", onehot, values_in.reshape(tile_count, ROWS, NTR),
                          precision=lax.Precision.HIGHEST)
        return (sums / children[:, :, None]).reshape(tile_count * COARSE, NTR)

    def prolong(coarse_values):
        spread = jnp.einsum("tic,tcn->tin", onehot, coarse_values.reshape(tile_count, COARSE, NTR),
                            precision=lax.Precision.HIGHEST)
        return spread.reshape(CELLS, NTR)

    fine_ends = []
    for slice_index in range(SLICES):
        tracer_state = starts[slice_index]
        for step_index in range(STEPS):
            tracer_state = fine_step(tracer_state, sources, fine_ops[slice_index],
                                     col_index[slice_index], live_count[slice_index])
        fine_ends.append(tracer_state)
    coarse_state = jnp.zeros((tile_count * COARSE, NTR), jnp.float32)
    outputs = []
    for slice_index in range(SLICES):
        if slice_index + 1 < SLICES:
            following = starts[slice_index + 1]
        else:
            following = jnp.zeros((CELLS, NTR), jnp.float32)
        jump_term = restrict(fine_ends[slice_index] - following)
        coarse_image = coarse_apply(coarse_state, coarse_op)
        outputs.append(fine_ends[slice_index] + prolong(coarse_image))
        coarse_state = coarse_image + jump_term
    return jnp.stack(outputs)
```

```python
import jax
import jax.numpy as jnp
from jax import lax
from jax.experimental import pallas as pl
from jax.experimental.pallas import tpu as pltpu
from jax.sharding import PartitionSpec as P

HALO = 256
BS = 128
F32 = jnp.float32
BF16 = jnp.bfloat16
VMEM = pl.BlockSpec(memory_space=pltpu.VMEM)
SMEM = pl.BlockSpec(memory_space=pltpu.SMEM)


def call(kernel, outs, in_specs, flops, nbytes, scratch=()):
    return pl.pallas_call(
        kernel,
        out_shape=[jax.ShapeDtypeStruct(shape, dtype) for shape, dtype in outs],
        in_specs=in_specs,
        out_specs=[VMEM] * len(outs),
        scratch_shapes=list(scratch),
        cost_estimate=pl.CostEstimate(flops=flops, bytes_accessed=nbytes, transcendentals=0),
        compiler_params=pltpu.CompilerParams(vmem_limit_bytes=40 << 20),
    )


def halves(value):
    high = value.astype(BF16)
    return high, (value - high.astype(F32)).astype(BF16)


def pair(value):
    return jnp.concatenate(halves(value), axis=1)


def dot(a, b):
    return jnp.dot(a, b, preferred_element_type=F32)


def folded(product):
    width = product.shape[1] // 2
    return product[:, :width] + product[:, width:]


def prepare(live_ref, ops_ref, map_ref, starts_ref, coarse_ref,
            high_ref, low_ref, gather_ref, spread_ref, inverse_ref, own_ref, rstart_ref, coarse2_ref):
    blocks, slots = ops_ref.shape[:2]
    coarse = coarse_ref.shape[0]
    for b in range(blocks):
        for k in range(slots):
            high, low = halves(jnp.where(k < live_ref[b], ops_ref[b, k], 0.0))
            high_ref[b, :, k * BS:(k + 1) * BS] = high
            low_ref[b, :, k * BS:(k + 1) * BS] = low
        own_ref[b * BS:(b + 1) * BS, :] = pair(starts_ref[b * BS:(b + 1) * BS, :])
    cells = lax.broadcasted_iota(jnp.int32, (coarse, BS), 0)
    children = jnp.zeros((coarse, 1), F32)
    for b in range(blocks):
        chosen = jnp.where(map_ref[b:b + 1, :] == cells, 1.0, 0.0)
        children = children + jnp.sum(chosen, axis=1, keepdims=True)
        gather_ref[:, b * BS:(b + 1) * BS] = chosen.astype(BF16)
        spread_ref[b * BS:(b + 1) * BS, :] = chosen.T.astype(BF16)
    inverse = jnp.broadcast_to(1.0 / children, inverse_ref.shape)
    inverse_ref[...] = inverse
    rstart_ref[...] = folded(dot(gather_ref[...], own_ref[...])) * inverse
    width = coarse_ref.shape[1]
    high, low = halves(coarse_ref[...])
    coarse2_ref[:, :width] = high
    coarse2_ref[:, width:] = low


def transport(cols_ref, high_ref, low_ref, own_ref, before_ref, after_ref, sources_ref, window, emit):
    rows = own_ref.shape[0]
    blocks = high_ref.shape[0]
    slots = high_ref.shape[2] // BS
    window[0:HALO, :] = pair(before_ref[...])
    window[HALO:HALO + rows, :] = own_ref[...]
    window[HALO + rows:, :] = pair(after_ref[...])
    for b in range(blocks):
        pieces = []
        for k in range(slots):
            at = pl.multiple_of(cols_ref[b * slots + k] * BS, BS)
            pieces.append(window[pl.ds(at, BS), :])
        pieces = jnp.concatenate(pieces, axis=0)
        tracers = pieces.shape[1] // 2
        value = folded(dot(high_ref[b], pieces)) + dot(low_ref[b], pieces[:, :tracers])
        emit(b, value + sources_ref[b * BS:(b + 1) * BS, :])


def first_step(cols_ref, high_ref, low_ref, own_ref, before_ref, after_ref, sources_ref,
               next_ref, head_ref, tail_ref, window):
    blocks = high_ref.shape[0]
    ends = HALO // BS

    def emit(b, value):
        next_ref[b * BS:(b + 1) * BS, :] = pair(value)
        if b < ends:
            head_ref[b * BS:(b + 1) * BS, :] = value
        if b >= blocks - ends:
            at = b - blocks + ends
            tail_ref[at * BS:(at + 1) * BS, :] = value

    transport(cols_ref, high_ref, low_ref, own_ref, before_ref, after_ref, sources_ref, window, emit)


def second_step(cols_ref, high_ref, low_ref, own_ref, before_ref, after_ref, sources_ref,
                gather_ref, inverse_ref, following_ref,
                end_ref, jump_ref, head_ref, tail_ref, window, split):
    def emit(b, value):
        end_ref[b * BS:(b + 1) * BS, :] = value
        split[b * BS:(b + 1) * BS, :] = pair(value)

    transport(cols_ref, high_ref, low_ref, own_ref, before_ref, after_ref, sources_ref, window, emit)
    jump = folded(dot(gather_ref[...], split[...])) * inverse_ref[...] - following_ref[...]
    rim = head_ref.shape[0]
    jump_ref[...] = jump
    head_ref[...] = jump[:rim]
    tail_ref[...] = jump[jump.shape[0] - rim:]


def coarse_product(coarse2_ref, before_ref, own_ref, after_ref):
    width = coarse2_ref.shape[1] // 2
    extended = jnp.concatenate([pair(before_ref[...]), pair(own_ref[...]), pair(after_ref[...])], axis=0)
    tracers = extended.shape[1] // 2
    return folded(dot(coarse2_ref[:, :width], extended)) + dot(coarse2_ref[:, width:], extended[:, :tracers])


def advance(coarse2_ref, before_ref, own_ref, after_ref, jump_ref, image_ref,
            state_ref, head_ref, tail_ref, total_ref):
    image = coarse_product(coarse2_ref, before_ref, own_ref, after_ref)
    state = image + jump_ref[...]
    rim = head_ref.shape[0]
    head_ref[...] = state[:rim]
    tail_ref[...] = state[state.shape[0] - rim:]
    state_ref[...] = state
    total_ref[...] = image_ref[...] + image


def finish(coarse2_ref, before_ref, own_ref, after_ref, image_ref, spread_ref, end_ref, out_ref):
    image = image_ref[...] + coarse_product(coarse2_ref, before_ref, own_ref, after_ref)
    split = pair(image)
    for b in range(end_ref.shape[0] // BS):
        rows = slice(b * BS, (b + 1) * BS)
        out_ref[rows, :] = end_ref[rows, :] + folded(dot(spread_ref[rows, :], split))


def ring_pair(head, tail, axis):
    count = lax.axis_size(axis)
    before = lax.ppermute(tail, axis, [(i, (i + 1) % count) for i in range(count)])
    after = lax.ppermute(head, axis, [((i + 1) % count, i) for i in range(count)])
    return before, after


def on_device(starts, sources, fine_ops, col_index, live_count, coarse_op, cell_map):
    first_state = starts[0]
    transport_ops = fine_ops[0]
    rows, tracers = first_state.shape
    blocks, slots = transport_ops.shape[:2]
    columns = col_index[0].reshape(-1)
    live = live_count[0]
    coarse, reach = coarse_op.shape
    rim = (reach - coarse) // 2
    slices = lax.axis_size("tm")
    tiles = lax.axis_size("tile")
    window = rows + 2 * HALO
    step_flops = 6 * rows * slots * BS * tracers
    coarse_flops = 6 * coarse * reach * tracers

    before, after = ring_pair(first_state[:HALO], first_state[rows - HALO:], "tile")
    high, low, gather, spread, inverse, own, rstart, coarse2 = call(
        prepare,
        [((blocks, BS, slots * BS), BF16), ((blocks, BS, slots * BS), BF16), ((coarse, rows), BF16),
         ((rows, coarse), BF16), ((coarse, tracers), F32), ((rows, 2 * tracers), BF16),
         ((coarse, tracers), F32), ((coarse, 2 * reach), BF16)],
        [SMEM, VMEM, VMEM, VMEM, VMEM], 4 * coarse * rows * tracers, 14_000_000,
    )(live, transport_ops, cell_map.reshape(-1, BS), first_state, coarse_op)
    following = lax.ppermute(rstart, "tm", [(i + 1, i) for i in range(slices - 1)])

    step_in = [SMEM] + [VMEM] * 6
    state, head, tail = call(
        first_step,
        [((rows, 2 * tracers), BF16), ((HALO, tracers), F32), ((HALO, tracers), F32)],
        step_in, step_flops, 6_000_000, [pltpu.VMEM((window, 2 * tracers), BF16)],
    )(columns, high, low, own, before, after, sources)
    before, after = ring_pair(head, tail, "tile")
    fine_end, jump, head, tail = call(
        second_step,
        [((rows, tracers), F32), ((coarse, tracers), F32), ((rim, tracers), F32), ((rim, tracers), F32)],
        step_in + [VMEM] * 3, step_flops + 4 * coarse * rows * tracers, 8_000_000,
        [pltpu.VMEM((window, 2 * tracers), BF16), pltpu.VMEM((rows, 2 * tracers), BF16)],
    )(columns, high, low, state, before, after, sources, gather, inverse, following)

    def to_slice(block, n, shift):
        route = [((n - 1) * tiles + i, n * tiles + (i + shift) % tiles) for i in range(tiles)]
        return lax.ppermute(block, ("tm", "tile"), route)

    image = jnp.zeros((coarse, tracers), F32)
    state = jump
    for n in range(1, slices):
        before = to_slice(tail, n, 1)
        after = to_slice(head, n, -1)
        own = to_slice(state, n, 0)
        if n < slices - 1:
            state, head, tail, image = call(
                advance,
                [((coarse, tracers), F32), ((rim, tracers), F32), ((rim, tracers), F32), ((coarse, tracers), F32)],
                [VMEM] * 6, coarse_flops, 2_000_000,
            )(coarse2, before, own, after, jump, image)
        else:
            (result,) = call(
                finish, [((rows, tracers), F32)], [VMEM] * 7,
                coarse_flops + 4 * coarse * rows * tracers, 4_000_000,
            )(coarse2, before, own, after, image, spread, fine_end)
    return result[None]


def solution(mesh):
    placed = (
        P("tm", "tile", None),
        P("tile", None),
        P("tm", "tile", None, None, None),
        P("tm", "tile", None),
        P("tm", "tile"),
        P("tile", None),
        P("tile"),
    )
    return jax.shard_map(
        on_device, mesh=mesh, in_specs=placed, out_specs=P("tm", "tile", None), check_vma=False
    )
```

```python
import jax
import jax.numpy as jnp
from jax import lax
from jax.experimental import pallas as pl
from jax.experimental.pallas import tpu as pltpu
from jax.sharding import PartitionSpec as P


HALO = 256
BS = 128
F32 = jnp.float32
BF16 = jnp.bfloat16
VMEM = pl.BlockSpec(memory_space=pltpu.VMEM)
SMEM = pl.BlockSpec(memory_space=pltpu.SMEM)
HBM = pl.BlockSpec(memory_space=pltpu.HBM)


def call(kernel, outs, in_specs, flops, nbytes, scratch=()):
    return pl.pallas_call(
        kernel,
        out_shape=[jax.ShapeDtypeStruct(shape, dtype) for shape, dtype in outs],
        in_specs=in_specs,
        out_specs=[VMEM] * len(outs),
        scratch_shapes=list(scratch),
        cost_estimate=pl.CostEstimate(flops=flops, bytes_accessed=nbytes, transcendentals=0),
        compiler_params=pltpu.CompilerParams(vmem_limit_bytes=16 << 20),
    )


def kept(value):
    return pltpu.with_memory_space_constraint(value, pltpu.HBM)


def halves(value):
    high = value.astype(BF16)
    return high, (value - high.astype(F32)).astype(BF16)


def pair(value):
    return jnp.concatenate(halves(value), axis=1)


def dot(a, b):
    return jnp.dot(a, b, preferred_element_type=F32)


def folded(product):
    width = product.shape[1] // 2
    return product[:, :width] + product[:, width:]


def odd_tile():
    return lax.rem(lax.axis_index("tile"), 2)


def ends(starts_ref, far_ref, near_ref, sems):
    last = starts_ref.shape[0] - HALO
    odd = odd_tile()
    copies = [
        pltpu.make_async_copy(
            starts_ref.at[pl.ds(pl.multiple_of(side * last, BS), HALO), :], out_ref, sems.at[index]
        )
        for index, (side, out_ref) in enumerate(((odd, far_ref), (1 - odd, near_ref)))
    ]
    for copy in copies:
        copy.start()
    for copy in copies:
        copy.wait()


def run_copies(copies):
    for copy in copies:
        copy.start()
    return copies


def fetch(ops_ref, starts_ref, sources_ref, ops_out, own_ref, sources_out, held, sems):
    copies = run_copies([
        pltpu.make_async_copy(starts_ref, held, sems.at[0]),
        pltpu.make_async_copy(ops_ref, ops_out, sems.at[1]),
        pltpu.make_async_copy(sources_ref, sources_out, sems.at[2]),
    ])
    copies[0].wait()
    for b in range(held.shape[0] // BS):
        own_ref[b * BS:(b + 1) * BS, :] = pair(held[b * BS:(b + 1) * BS, :])
    for copy in copies[1:]:
        copy.wait()


def prepare(map_hbm, coarse_hbm, own_ref, token_ref,
            gather_ref, spread_ref, inverse_ref, rstart_ref, coarse2_ref, map_ref, coarse_ref, sems):
    copies = run_copies([
        pltpu.make_async_copy(map_hbm, map_ref, sems.at[0]),
        pltpu.make_async_copy(coarse_hbm, coarse_ref, sems.at[1]),
    ])
    copies[0].wait()
    coarse = coarse_ref.shape[0]
    cells = lax.broadcasted_iota(jnp.int32, (coarse, BS), 0)
    children = jnp.zeros((coarse, 1), F32)
    for b in range(map_ref.shape[0]):
        chosen = jnp.where(map_ref[b:b + 1, :] == cells, 1.0, 0.0)
        children = children + jnp.sum(chosen, axis=1, keepdims=True)
        gather_ref[:, b * BS:(b + 1) * BS] = chosen.astype(BF16)
        spread_ref[b * BS:(b + 1) * BS, :] = chosen.T.astype(BF16)
    inverse = jnp.broadcast_to(1.0 / children, inverse_ref.shape)
    inverse_ref[...] = inverse
    rstart_ref[...] = folded(dot(gather_ref[...], own_ref[...])) * inverse
    copies[1].wait()
    width = coarse_ref.shape[1]
    high, low = halves(coarse_ref[...])
    coarse2_ref[:, :width] = high
    coarse2_ref[:, width:] = low


def transport(cols_hbm, live_hbm, ops_ref, own_ref, far_ref, near_ref, sources_ref,
              cols_ref, live_ref, window, sems, emit):
    copies = run_copies([
        pltpu.make_async_copy(cols_hbm, cols_ref, sems.at[0]),
        pltpu.make_async_copy(live_hbm, live_ref, sems.at[1]),
    ])
    rows = own_ref.shape[0]
    blocks, slots = ops_ref.shape[:2]
    odd = odd_tile()
    window[pl.ds(pl.multiple_of(odd * (HALO + rows), BS), HALO), :] = pair(far_ref[...])
    window[pl.ds(pl.multiple_of((1 - odd) * (HALO + rows), BS), HALO), :] = pair(near_ref[...])
    window[HALO:HALO + rows, :] = own_ref[...]
    for copy in copies:
        copy.wait()
    for b in range(blocks):
        pieces, highs, lows = [], [], []
        for k in range(slots):
            at = pl.multiple_of(cols_ref[k, b] * BS, BS)
            pieces.append(window[pl.ds(at, BS), :])
            high, low = halves(jnp.where(k < live_ref[0, b], ops_ref[b, k], 0.0))
            highs.append(high)
            lows.append(low)
        pieces = jnp.concatenate(pieces, axis=0)
        tracers = pieces.shape[1] // 2
        value = folded(dot(jnp.concatenate(highs, axis=1), pieces))
        value = value + dot(jnp.concatenate(lows, axis=1), pieces[:, :tracers])
        emit(b, value + sources_ref[b * BS:(b + 1) * BS, :])


def sides(block, far_ref, near_ref, width):
    odd = odd_tile()
    last = block.shape[0] - width
    far_ref[...] = block[pl.ds(pl.multiple_of(odd * last, 64), width), :]
    near_ref[...] = block[pl.ds(pl.multiple_of((1 - odd) * last, 64), width), :]


def first_step(cols_hbm, live_hbm, ops_ref, own_ref, far_ref, near_ref, sources_ref,
               next_ref, nfar_ref, nnear_ref, token_ref, cols_ref, live_ref, window, sems, rims):
    blocks = ops_ref.shape[0]
    side = HALO // BS

    def emit(b, value):
        next_ref[b * BS:(b + 1) * BS, :] = pair(value)
        if b < side:
            rims[b * BS:(b + 1) * BS, :] = value
        if b >= blocks - side:
            at = b - blocks + 2 * side
            rims[at * BS:(at + 1) * BS, :] = value

    transport(cols_hbm, live_hbm, ops_ref, own_ref, far_ref, near_ref, sources_ref,
              cols_ref, live_ref, window, sems, emit)
    sides(rims, nfar_ref, nnear_ref, HALO)
    token_ref[...] = jnp.zeros_like(token_ref)


def second_step(cols_hbm, live_hbm, ops_ref, own_ref, far_ref, near_ref, sources_ref,
                gather_ref, inverse_ref, following_ref,
                end_ref, jump_ref, nfar_ref, nnear_ref, cols_ref, live_ref, window, sems, split):
    def emit(b, value):
        end_ref[b * BS:(b + 1) * BS, :] = value
        split[b * BS:(b + 1) * BS, :] = pair(value)

    transport(cols_hbm, live_hbm, ops_ref, own_ref, far_ref, near_ref, sources_ref,
              cols_ref, live_ref, window, sems, emit)
    jump_ref[...] = folded(dot(gather_ref[...], split[...])) * inverse_ref[...] - following_ref[...]
    sides(jump_ref, nfar_ref, nnear_ref, nfar_ref.shape[0])


def coarse_product(coarse2_ref, far_ref, own_ref, near_ref, window):
    width = coarse2_ref.shape[1] // 2
    rim, rows = far_ref.shape[0], own_ref.shape[0]
    odd = odd_tile()
    window[pl.ds(pl.multiple_of(odd * (rim + rows), 64), rim), :] = pair(far_ref[...])
    window[pl.ds(pl.multiple_of((1 - odd) * (rim + rows), 64), rim), :] = pair(near_ref[...])
    window[rim:rim + rows, :] = pair(own_ref[...])
    tracers = own_ref.shape[1]
    product = folded(dot(coarse2_ref[:, :width], window[...]))
    return product + dot(coarse2_ref[:, width:], window[:, :tracers])


def advance(coarse2_ref, far_ref, own_ref, near_ref, jump_ref, later_ref, *refs):
    state_ref, nfar_ref, nnear_ref, total_ref, window = refs[-5:]
    image = coarse_product(coarse2_ref, far_ref, own_ref, near_ref, window)
    state_ref[...] = image + (jump_ref[...] - later_ref[...])
    sides(state_ref, nfar_ref, nnear_ref, nfar_ref.shape[0])
    total_ref[...] = image if len(refs) == 5 else refs[0][...] + image


def finish(coarse2_ref, far_ref, own_ref, near_ref, image_ref, spread_ref, end_ref, out_ref, window):
    image = image_ref[...] + coarse_product(coarse2_ref, far_ref, own_ref, near_ref, window)
    split = pair(image)
    for b in range(end_ref.shape[0] // BS):
        rows = slice(b * BS, (b + 1) * BS)
        out_ref[rows, :] = end_ref[rows, :] + folded(dot(spread_ref[rows, :], split))


def swapped(far, near):
    count = lax.axis_size("tile")
    far = lax.ppermute(far, "tile", [(i, (i + 1 if i % 2 else i - 1) % count) for i in range(count)])
    near = lax.ppermute(near, "tile", [(i, i ^ 1) for i in range(count)])
    return far, near


def on_device(starts, sources, fine_ops, col_index, live_count, coarse_op, cell_map):
    first_state = starts[0]
    ops = fine_ops[0]
    rows, tracers = first_state.shape
    blocks, slots = ops.shape[:2]
    columns = col_index[0].T
    live = live_count
    coarse, reach = coarse_op.shape
    rim = (reach - coarse) // 2
    slices = lax.axis_size("tm")
    tiles = lax.axis_size("tile")
    window = pltpu.VMEM((rows + 2 * HALO, 2 * tracers), BF16)
    step_flops = 6 * rows * slots * BS * tracers
    coarse_flops = 6 * coarse * reach * tracers
    side = ((HALO, tracers), F32)
    coarse_rim = ((rim, tracers), F32)
    coarse_all = ((coarse, tracers), F32)

    far, near = call(ends, [side, side], [HBM], 0, 500_000, [pltpu.SemaphoreType.DMA((2,))])(kept(first_state))
    far, near = swapped(far, near)
    ops, own, sources = call(
        fetch, [(ops.shape, F32), ((rows, 2 * tracers), BF16), (sources.shape, F32)],
        [HBM] * 3, 0, 9_000_000, [pltpu.VMEM((rows, tracers), F32), pltpu.SemaphoreType.DMA((3,))],
    )(kept(ops), kept(first_state), kept(sources))

    step_in = [HBM] * 2 + [VMEM] * 5
    step_scratch = [pltpu.SMEM(columns.shape, jnp.int32), pltpu.SMEM(live.shape, jnp.int32), window,
                    pltpu.SemaphoreType.DMA((2,))]
    state, far, near, token = call(
        first_step, [((rows, 2 * tracers), BF16), side, side, ((8, tracers), F32)],
        step_in, step_flops, 6_000_000, step_scratch + [pltpu.VMEM((2 * HALO, tracers), F32)],
    )(kept(columns), kept(live), ops, own, far, near, sources)
    far, near = swapped(far, near)
    gather, spread, inverse, rstart, coarse2 = call(
        prepare,
        [((coarse, rows), BF16), ((rows, coarse), BF16), coarse_all, coarse_all, ((coarse, 2 * reach), BF16)],
        [HBM] * 2 + [VMEM, VMEM], 4 * coarse * rows * tracers, 6_000_000,
        [pltpu.VMEM((blocks, BS), jnp.int32), pltpu.VMEM((coarse, reach), F32), pltpu.SemaphoreType.DMA((2,))],
    )(kept(cell_map.reshape(-1, BS)), kept(coarse_op), own, token)
    following = lax.ppermute(rstart, "tm", [(1, 0)])
    later = lax.ppermute(rstart, "tm", [(i + 1, i) for i in range(1, slices - 1)])
    fine_end, jump, far, near = call(
        second_step, [((rows, tracers), F32), coarse_all, coarse_rim, coarse_rim],
        step_in + [VMEM] * 3, step_flops + 4 * coarse * rows * tracers, 8_000_000,
        step_scratch + [pltpu.VMEM((rows, 2 * tracers), BF16)],
    )(kept(columns), kept(live), ops, state, far, near, sources, gather, inverse, following)

    def to_slice(block, n, target):
        route = [((n - 1) * tiles + i, n * tiles + target(i) % tiles) for i in range(tiles)]
        return lax.ppermute(block, ("tm", "tile"), route)

    image = ()
    state = jump
    coarse_window = [pltpu.VMEM((reach, 2 * tracers), BF16)]
    for n in range(1, slices):
        far = to_slice(far, n, lambda i: i + 1 if i % 2 else i - 1)
        near = to_slice(near, n, lambda i: i ^ 1)
        own = to_slice(state, n, lambda i: i)
        if n < slices - 1:
            state, far, near, *image = call(
                advance, [coarse_all, coarse_rim, coarse_rim, coarse_all],
                [VMEM] * (6 + len(image)), coarse_flops, 2_000_000, coarse_window,
            )(coarse2, far, own, near, jump, later, *image)
        else:
            (result,) = call(
                finish, [((rows, tracers), F32)], [VMEM] * 7,
                coarse_flops + 4 * coarse * rows * tracers, 4_000_000, coarse_window,
            )(coarse2, far, own, near, *image, spread, fine_end)
    return result[None]


def solution(mesh):
    placed = (
        P("tm", "tile", None),
        P("tile", None),
        P("tm", "tile", None, None, None),
        P("tm", "tile", None),
        P("tm", "tile"),
        P("tile", None),
        P("tile"),
    )

    return jax.shard_map(on_device, mesh=mesh, in_specs=placed, out_specs=P("tm", "tile", None), check_vma=False)
```

```python
import jax
import jax.numpy as jnp
from jax import lax
from jax.experimental import pallas as pl
from jax.experimental.pallas import tpu as pltpu
from jax.sharding import PartitionSpec as P


HALO = 256
BS = 128
F32 = jnp.float32
BF16 = jnp.bfloat16
VMEM = pl.BlockSpec(memory_space=pltpu.VMEM)
SMEM = pl.BlockSpec(memory_space=pltpu.SMEM)
HBM = pl.BlockSpec(memory_space=pltpu.HBM)


def call(kernel, outs, in_specs, flops, nbytes, scratch=(), out_spec=VMEM, aliases=None):
    return pl.pallas_call(
        kernel,
        out_shape=[jax.ShapeDtypeStruct(shape, dtype) for shape, dtype in outs],
        in_specs=in_specs,
        out_specs=[out_spec] * len(outs),
        input_output_aliases=aliases or {},
        scratch_shapes=list(scratch),
        cost_estimate=pl.CostEstimate(flops=flops, bytes_accessed=nbytes, transcendentals=0),
        compiler_params=pltpu.CompilerParams(vmem_limit_bytes=16 << 20),
    )


def kept(value):
    return pltpu.with_memory_space_constraint(value, pltpu.HBM)


def halves(value):
    high = value.astype(BF16)
    return high, (value - high.astype(F32)).astype(BF16)


def pair(value):
    return jnp.concatenate(halves(value), axis=1)


def dot(a, b):
    return jnp.dot(a, b, preferred_element_type=F32)


def folded(product):
    width = product.shape[1] // 2
    return product[:, :width] + product[:, width:]


def odd_tile():
    return lax.rem(lax.axis_index("tile"), 2)


def ends(starts_ref, far_ref, near_ref, sems):
    last = starts_ref.shape[0] - HALO
    odd = odd_tile()
    copies = [
        pltpu.make_async_copy(
            starts_ref.at[pl.ds(pl.multiple_of(side * last, BS), HALO), :], out_ref, sems.at[index]
        )
        for index, (side, out_ref) in enumerate(((odd, far_ref), (1 - odd, near_ref)))
    ]
    for copy in copies:
        copy.start()
    for copy in copies:
        copy.wait()


def run_copies(copies):
    for copy in copies:
        copy.start()
    return copies


def fetch(ops_ref, starts_ref, sources_ref, ops_out, own_ref, sources_out, held, sems):
    copies = run_copies([
        pltpu.make_async_copy(starts_ref, held, sems.at[0]),
        pltpu.make_async_copy(ops_ref, ops_out, sems.at[1]),
        pltpu.make_async_copy(sources_ref, sources_out, sems.at[2]),
    ])
    copies[0].wait()
    for b in range(held.shape[0] // BS):
        own_ref[b * BS:(b + 1) * BS, :] = pair(held[b * BS:(b + 1) * BS, :])
    for copy in copies[1:]:
        copy.wait()


def prepare(map_hbm, own_ref, token_ref, gather_ref, inverse_ref, rstart_ref, map_ref, sems):
    copy = pltpu.make_async_copy(map_hbm, map_ref, sems.at[0])
    copy.start()
    copy.wait()
    coarse = gather_ref.shape[0]
    cells = lax.broadcasted_iota(jnp.int32, (coarse, BS), 0)
    children = jnp.zeros((coarse, 1), F32)
    for b in range(map_ref.shape[0]):
        chosen = jnp.where(map_ref[b:b + 1, :] == cells, 1.0, 0.0)
        children = children + jnp.sum(chosen, axis=1, keepdims=True)
        gather_ref[:, b * BS:(b + 1) * BS] = chosen.astype(BF16)
    inverse = jnp.broadcast_to(1.0 / children, inverse_ref.shape)
    inverse_ref[...] = inverse
    rstart_ref[...] = folded(dot(gather_ref[...], own_ref[...])) * inverse


def prepare_late(coarse_hbm, gather_ref, token_ref, spread_ref, coarse2_ref, coarse_ref, sems):
    copy = pltpu.make_async_copy(coarse_hbm, coarse_ref, sems.at[0])
    copy.start()
    for b in range(gather_ref.shape[1] // BS):
        spread_ref[b * BS:(b + 1) * BS, :] = gather_ref[:, b * BS:(b + 1) * BS].astype(F32).T.astype(BF16)
    copy.wait()
    width = coarse_ref.shape[1]
    high, low = halves(coarse_ref[...])
    coarse2_ref[:, :width] = high
    coarse2_ref[:, width:] = low


def transport(cols_hbm, live_hbm, ops_ref, own_ref, far_ref, near_ref, sources_ref,
              cols_ref, live_ref, window, sems, emit):
    copies = run_copies([
        pltpu.make_async_copy(cols_hbm, cols_ref, sems.at[0]),
        pltpu.make_async_copy(live_hbm, live_ref, sems.at[1]),
    ])
    rows = own_ref.shape[0]
    blocks, slots = ops_ref.shape[:2]
    odd = odd_tile()
    window[pl.ds(pl.multiple_of(odd * (HALO + rows), BS), HALO), :] = pair(far_ref[...])
    window[pl.ds(pl.multiple_of((1 - odd) * (HALO + rows), BS), HALO), :] = pair(near_ref[...])
    window[HALO:HALO + rows, :] = own_ref[...]
    for copy in copies:
        copy.wait()
    for b in range(blocks):
        pieces, highs, lows = [], [], []
        for k in range(slots):
            at = pl.multiple_of(cols_ref[k, b] * BS, BS)
            pieces.append(window[pl.ds(at, BS), :])
            high, low = halves(jnp.where(k < live_ref[0, b], ops_ref[b, k], 0.0))
            highs.append(high)
            lows.append(low)
        pieces = jnp.concatenate(pieces, axis=0)
        tracers = pieces.shape[1] // 2
        value = folded(dot(jnp.concatenate(highs, axis=1), pieces))
        value = value + dot(jnp.concatenate(lows, axis=1), pieces[:, :tracers])
        emit(b, value + sources_ref[b * BS:(b + 1) * BS, :])


def sides(block, far_ref, near_ref, width):
    odd = odd_tile()
    last = block.shape[0] - width
    far_ref[...] = block[pl.ds(pl.multiple_of(odd * last, 64), width), :]
    near_ref[...] = block[pl.ds(pl.multiple_of((1 - odd) * last, 64), width), :]


def first_step(cols_hbm, live_hbm, ops_ref, own_ref, far_ref, near_ref, sources_ref,
               next_ref, nfar_ref, nnear_ref, token_ref, cols_ref, live_ref, window, sems, rims):
    blocks = ops_ref.shape[0]
    side = HALO // BS

    def emit(b, value):
        next_ref[b * BS:(b + 1) * BS, :] = pair(value)
        if b < side:
            rims[b * BS:(b + 1) * BS, :] = value
        if b >= blocks - side:
            at = b - blocks + 2 * side
            rims[at * BS:(at + 1) * BS, :] = value

    transport(cols_hbm, live_hbm, ops_ref, own_ref, far_ref, near_ref, sources_ref,
              cols_ref, live_ref, window, sems, emit)
    sides(rims, nfar_ref, nnear_ref, HALO)
    token_ref[...] = jnp.zeros_like(token_ref)


def restricted_step(refs, gather_ref, inverse_ref, end_ref, jump_ref, cols_ref, live_ref, window, sems, split):
    def emit(b, value):
        end_ref[b * BS:(b + 1) * BS, :] = value
        split[b * BS:(b + 1) * BS, :] = pair(value)

    transport(*refs, cols_ref, live_ref, window, sems, emit)
    jump_ref[...] = folded(dot(gather_ref[...], split[...])) * inverse_ref[...]


def second_step_first(*refs):
    operands, (gather_ref, inverse_ref, following_ref) = refs[:7], refs[7:10]
    end_ref, jump_ref, nfar_ref, nnear_ref = refs[10:14]

    @pl.when(lax.axis_index("tm") == 0)
    def _():
        restricted_step(operands, gather_ref, inverse_ref, end_ref, jump_ref, *refs[14:])
        jump_ref[...] = jump_ref[...] - following_ref[...]
        sides(jump_ref, nfar_ref, nnear_ref, nfar_ref.shape[0])


def second_step_rest(*refs):
    operands, (gather_ref, inverse_ref) = refs[:7], refs[7:9]
    end_ref, jump_ref = refs[10:12]
    first = lax.axis_index("tm") == 0

    @pl.when(first)
    def _():
        jump_ref[...] = jnp.zeros_like(jump_ref)

    @pl.when(jnp.logical_not(first))
    def _():
        restricted_step(operands, gather_ref, inverse_ref, end_ref, jump_ref, *refs[12:])


def coarse_product(coarse2_ref, far_ref, own_ref, near_ref, window):
    width = coarse2_ref.shape[1] // 2
    rim, rows = far_ref.shape[0], own_ref.shape[0]
    odd = odd_tile()
    window[pl.ds(pl.multiple_of(odd * (rim + rows), 64), rim), :] = pair(far_ref[...])
    window[pl.ds(pl.multiple_of((1 - odd) * (rim + rows), 64), rim), :] = pair(near_ref[...])
    window[rim:rim + rows, :] = pair(own_ref[...])
    tracers = own_ref.shape[1]
    product = folded(dot(coarse2_ref[:, :width], window[...]))
    return product + dot(coarse2_ref[:, width:], window[:, :tracers])


def advance(coarse2_ref, far_ref, own_ref, near_ref, jump_ref, later_ref, *refs):
    state_ref, nfar_ref, nnear_ref, total_ref, window = refs[-5:]
    image = coarse_product(coarse2_ref, far_ref, own_ref, near_ref, window)
    state_ref[...] = image + (jump_ref[...] - later_ref[...])
    sides(state_ref, nfar_ref, nnear_ref, nfar_ref.shape[0])
    total_ref[...] = image if len(refs) == 5 else refs[0][...] + image


def finish(coarse2_ref, far_ref, own_ref, near_ref, image_ref, spread_ref, end_ref, out_hbm, window, held, sems):
    image = image_ref[...] + coarse_product(coarse2_ref, far_ref, own_ref, near_ref, window)
    split = pair(image)
    copies = []
    for b in range(sems.shape[0]):
        part = end_ref.shape[0] // sems.shape[0]
        rows = slice(b * part, (b + 1) * part)
        held[rows, :] = end_ref[rows, :] + folded(dot(spread_ref[rows, :], split))
        copies.append(pltpu.make_async_copy(held.at[rows, :], out_hbm.at[rows, :], sems.at[b]))
        copies[-1].start()
    for copy in copies:
        copy.wait()


def swapped(far, near):
    count = lax.axis_size("tile")
    far = lax.ppermute(far, "tile", [(i, (i + 1 if i % 2 else i - 1) % count) for i in range(count)])
    near = lax.ppermute(near, "tile", [(i, i ^ 1) for i in range(count)])
    return far, near


def on_device(starts, sources, fine_ops, col_index, live_count, coarse_op, cell_map):
    first_state = starts[0]
    ops = fine_ops[0]
    rows, tracers = first_state.shape
    blocks, slots = ops.shape[:2]
    columns = col_index[0].T
    live = live_count
    coarse, reach = coarse_op.shape
    rim = (reach - coarse) // 2
    slices = lax.axis_size("tm")
    tiles = lax.axis_size("tile")
    window = pltpu.VMEM((rows + 2 * HALO, 2 * tracers), BF16)
    step_flops = 6 * rows * slots * BS * tracers
    coarse_flops = 6 * coarse * reach * tracers
    side = ((HALO, tracers), F32)
    coarse_rim = ((rim, tracers), F32)
    coarse_all = ((coarse, tracers), F32)

    far, near = call(ends, [side, side], [HBM], 0, 500_000, [pltpu.SemaphoreType.DMA((2,))])(kept(first_state))
    far, near = swapped(far, near)
    ops, own, sources = call(
        fetch, [(ops.shape, F32), ((rows, 2 * tracers), BF16), (sources.shape, F32)],
        [HBM] * 3, 0, 9_000_000, [pltpu.VMEM((rows, tracers), F32), pltpu.SemaphoreType.DMA((3,))],
    )(kept(ops), kept(first_state), kept(sources))

    step_in = [HBM] * 2 + [VMEM] * 5
    step_scratch = [pltpu.SMEM(columns.shape, jnp.int32), pltpu.SMEM(live.shape, jnp.int32), window,
                    pltpu.SemaphoreType.DMA((2,))]
    state, far, near, token = call(
        first_step, [((rows, 2 * tracers), BF16), side, side, ((8, tracers), F32)],
        step_in, step_flops, 6_000_000, step_scratch + [pltpu.VMEM((2 * HALO, tracers), F32)],
    )(kept(columns), kept(live), ops, own, far, near, sources)
    far, near = swapped(far, near)
    gather, inverse, rstart = call(
        prepare, [((coarse, rows), BF16), coarse_all, coarse_all],
        [HBM, VMEM, VMEM], 4 * coarse * rows * tracers, 3_000_000,
        [pltpu.VMEM((blocks, BS), jnp.int32), pltpu.SemaphoreType.DMA((1,))],
    )(kept(cell_map.reshape(-1, BS)), own, token)
    following = lax.ppermute(rstart, "tm", [(1, 0)])
    later = lax.ppermute(rstart, "tm", [(i + 1, i) for i in range(1, slices - 1)])
    step_scratch = step_scratch + [pltpu.VMEM((rows, 2 * tracers), BF16)]
    step_args = (kept(columns), kept(live), ops, state, far, near, sources, gather, inverse)
    step_flops = step_flops + 4 * coarse * rows * tracers
    fine_end, jump, far, near = call(
        second_step_first, [((rows, tracers), F32), coarse_all, coarse_rim, coarse_rim],
        step_in + [VMEM] * 3, step_flops, 8_000_000, step_scratch,
    )(*step_args, following)

    def to_slice(block, n, target):
        route = [((n - 1) * tiles + i, n * tiles + target(i) % tiles) for i in range(tiles)]
        return lax.ppermute(block, ("tm", "tile"), route)

    image = ()
    state = jump
    coarse_window = [pltpu.VMEM((reach, 2 * tracers), BF16)]
    for n in range(1, slices):
        far = to_slice(far, n, lambda i: i + 1 if i % 2 else i - 1)
        near = to_slice(near, n, lambda i: i ^ 1)
        own = to_slice(state, n, lambda i: i)
        if n == 1:
            fine_end, jump = call(
                second_step_rest, [((rows, tracers), F32), coarse_all],
                step_in + [VMEM] * 3, step_flops, 8_000_000, step_scratch, aliases={9: 0},
            )(*step_args, fine_end)
            spread, coarse2 = call(
                prepare_late, [((rows, coarse), BF16), ((coarse, 2 * reach), BF16)],
                [HBM] + [VMEM] * 2, 0, 4_000_000,
                [pltpu.VMEM((coarse, reach), F32), pltpu.SemaphoreType.DMA((1,))],
            )(kept(coarse_op), gather, token)
        if n < slices - 1:
            state, far, near, *image = call(
                advance, [coarse_all, coarse_rim, coarse_rim, coarse_all],
                [VMEM] * (6 + len(image)), coarse_flops, 2_000_000, coarse_window,
            )(coarse2, far, own, near, jump, later, *image)
        else:
            (result,) = call(
                finish, [((rows, tracers), F32)], [VMEM] * 7,
                coarse_flops + 4 * coarse * rows * tracers, 4_000_000,
                coarse_window + [pltpu.VMEM((rows, tracers), F32), pltpu.SemaphoreType.DMA((6,))], HBM,
            )(coarse2, far, own, near, *image, spread, fine_end)
    return result[None]


def solution(mesh):
    placed = (
        P("tm", "tile", None),
        P("tile", None),
        P("tm", "tile", None, None, None),
        P("tm", "tile", None),
        P("tm", "tile"),
        P("tile", None),
        P("tile"),
    )

    return jax.shard_map(on_device, mesh=mesh, in_specs=placed, out_specs=P("tm", "tile", None), check_vma=False)
```

```python
import jax
import jax.numpy as jnp
from jax import lax
from jax.experimental import pallas as pl
from jax.experimental.pallas import tpu as pltpu
from jax.sharding import PartitionSpec as P


HALO = 256
BS = 128
F32 = jnp.float32
BF16 = jnp.bfloat16
VMEM = pl.BlockSpec(memory_space=pltpu.VMEM)
SMEM = pl.BlockSpec(memory_space=pltpu.SMEM)
HBM = pl.BlockSpec(memory_space=pltpu.HBM)


def call(kernel, outs, in_specs, flops, nbytes, scratch=(), out_spec=VMEM, aliases=None):
    return pl.pallas_call(
        kernel,
        out_shape=[jax.ShapeDtypeStruct(shape, dtype) for shape, dtype in outs],
        in_specs=in_specs,
        out_specs=[out_spec] * len(outs),
        input_output_aliases=aliases or {},
        scratch_shapes=list(scratch),
        cost_estimate=pl.CostEstimate(flops=flops, bytes_accessed=nbytes, transcendentals=0),
        compiler_params=pltpu.CompilerParams(vmem_limit_bytes=16 << 20),
    )


def kept(value):
    return pltpu.with_memory_space_constraint(value, pltpu.HBM)


def halves(value):
    high = value.astype(BF16)
    return high, (value - high.astype(F32)).astype(BF16)


def pair(value):
    return jnp.concatenate(halves(value), axis=1)


def dot(a, b):
    return jnp.dot(a, b, preferred_element_type=F32)


def folded(product):
    width = product.shape[1] // 2
    return product[:, :width] + product[:, width:]


def folded_twice(product):
    half = folded(product)
    rows = half.shape[0] // 2
    return half[:rows] + half[rows:]


def odd_tile():
    return lax.rem(lax.axis_index("tile"), 2)


def ends(starts_ref, far_ref, near_ref, sems):
    last = starts_ref.shape[0] - HALO
    odd = odd_tile()
    copies = [
        pltpu.make_async_copy(
            starts_ref.at[pl.ds(pl.multiple_of(side * last, BS), HALO), :], out_ref, sems.at[index]
        )
        for index, (side, out_ref) in enumerate(((odd, far_ref), (1 - odd, near_ref)))
    ]
    for copy in copies:
        copy.start()
    for copy in copies:
        copy.wait()


def run_copies(copies):
    for copy in copies:
        copy.start()
    return copies


def fetch(ops_ref, starts_ref, sources_ref, ops_out, own_ref, sources_out, held, sems):
    copies = run_copies([
        pltpu.make_async_copy(starts_ref, held, sems.at[0]),
        pltpu.make_async_copy(ops_ref, ops_out, sems.at[1]),
        pltpu.make_async_copy(sources_ref, sources_out, sems.at[2]),
    ])
    copies[0].wait()
    for b in range(held.shape[0] // BS):
        own_ref[b * BS:(b + 1) * BS, :] = pair(held[b * BS:(b + 1) * BS, :])
    for copy in copies[1:]:
        copy.wait()


def prepare(map_hbm, own_ref, token_ref, gather_ref, inverse_ref, rstart_ref, map_ref, sems):
    copy = pltpu.make_async_copy(map_hbm, map_ref, sems.at[0])
    copy.start()
    copy.wait()
    coarse = gather_ref.shape[0]
    cells = lax.broadcasted_iota(jnp.int32, (coarse, BS), 0)
    children = jnp.zeros((coarse, 1), F32)
    for b in range(map_ref.shape[0]):
        chosen = jnp.where(map_ref[b:b + 1, :] == cells, 1.0, 0.0)
        children = children + jnp.sum(chosen, axis=1, keepdims=True)
        gather_ref[:, b * BS:(b + 1) * BS] = chosen.astype(BF16)
    inverse = jnp.broadcast_to(1.0 / children, inverse_ref.shape)
    inverse_ref[...] = inverse
    rstart_ref[...] = folded(dot(gather_ref[...], own_ref[...])) * inverse


def split_coarse(coarse_hbm, token_ref, coarse2_ref, coarse_ref, sems):
    copy = pltpu.make_async_copy(coarse_hbm, coarse_ref, sems.at[0])
    copy.start()
    copy.wait()
    rows = coarse_ref.shape[0]
    high, low = halves(coarse_ref[...])
    coarse2_ref[:rows, :] = high
    coarse2_ref[rows:, :] = low


def transport(cols_hbm, live_hbm, ops_ref, own_ref, far_ref, near_ref, sources_ref,
              cols_ref, live_ref, window, sems, emit):
    copies = run_copies([
        pltpu.make_async_copy(cols_hbm, cols_ref, sems.at[0]),
        pltpu.make_async_copy(live_hbm, live_ref, sems.at[1]),
    ])
    rows = own_ref.shape[0]
    blocks, slots = ops_ref.shape[:2]
    odd = odd_tile()
    window[pl.ds(pl.multiple_of(odd * (HALO + rows), BS), HALO), :] = pair(far_ref[...])
    window[pl.ds(pl.multiple_of((1 - odd) * (HALO + rows), BS), HALO), :] = pair(near_ref[...])
    window[HALO:HALO + rows, :] = own_ref[...]
    for copy in copies:
        copy.wait()
    for b in range(blocks):
        pieces, highs, lows = [], [], []
        for k in range(slots):
            at = pl.multiple_of(cols_ref[k, b] * BS, BS)
            pieces.append(window[pl.ds(at, BS), :])
            high, low = halves(jnp.where(k < live_ref[0, b], ops_ref[b, k], 0.0))
            highs.append(high)
            lows.append(low)
        pieces = jnp.concatenate(pieces, axis=0)
        operator = jnp.concatenate([jnp.concatenate(highs, axis=1), jnp.concatenate(lows, axis=1)], axis=0)
        value = folded_twice(dot(operator, pieces))
        emit(b, value + sources_ref[b * BS:(b + 1) * BS, :])


def sides(block, far_ref, near_ref, width):
    odd = odd_tile()
    last = block.shape[0] - width
    far_ref[...] = block[pl.ds(pl.multiple_of(odd * last, 64), width), :]
    near_ref[...] = block[pl.ds(pl.multiple_of((1 - odd) * last, 64), width), :]


def first_step(cols_hbm, live_hbm, ops_ref, own_ref, far_ref, near_ref, sources_ref,
               next_ref, nfar_ref, nnear_ref, token_ref, cols_ref, live_ref, window, sems, rims):
    blocks = ops_ref.shape[0]
    side = HALO // BS

    def emit(b, value):
        next_ref[b * BS:(b + 1) * BS, :] = pair(value)
        if b < side:
            rims[b * BS:(b + 1) * BS, :] = value
        if b >= blocks - side:
            at = b - blocks + 2 * side
            rims[at * BS:(at + 1) * BS, :] = value

    transport(cols_hbm, live_hbm, ops_ref, own_ref, far_ref, near_ref, sources_ref,
              cols_ref, live_ref, window, sems, emit)
    sides(rims, nfar_ref, nnear_ref, HALO)
    token_ref[...] = jnp.zeros_like(token_ref)


def restricted_step(refs, gather_ref, inverse_ref, end_ref, jump_ref, cols_ref, live_ref, window, sems, split):
    def emit(b, value):
        end_ref[b * BS:(b + 1) * BS, :] = value
        split[b * BS:(b + 1) * BS, :] = pair(value)

    transport(*refs, cols_ref, live_ref, window, sems, emit)
    jump_ref[...] = folded(dot(gather_ref[...], split[...])) * inverse_ref[...]


def second_step_first(*refs):
    operands, (gather_ref, inverse_ref, following_ref) = refs[:7], refs[7:10]
    end_ref, jump_ref, nfar_ref, nnear_ref = refs[10:14]

    @pl.when(lax.axis_index("tm") == 0)
    def _():
        restricted_step(operands, gather_ref, inverse_ref, end_ref, jump_ref, *refs[14:])
        jump_ref[...] = jump_ref[...] - following_ref[...]
        sides(jump_ref, nfar_ref, nnear_ref, nfar_ref.shape[0])


def second_step_rest(chosen, gather_ref, inverse_ref, operands, end_ref, jump_ref, scratch):
    @pl.when(jnp.logical_not(chosen))
    def _():
        jump_ref[...] = jnp.zeros_like(jump_ref)

    @pl.when(chosen)
    def _():
        restricted_step(operands, gather_ref, inverse_ref, end_ref, jump_ref, *scratch)


def second_step_one(*refs):
    second_step_rest(lax.axis_index("tm") == 1, refs[7], refs[8], refs[:7], refs[10], refs[11], refs[12:])


def second_step_others(*refs):
    second_step_rest(lax.axis_index("tm") > 1, refs[7], refs[8], refs[:7], refs[10], refs[11], refs[13:])
    gather_ref, spread_ref = refs[7], refs[12]
    for b in range(gather_ref.shape[1] // BS):
        spread_ref[b * BS:(b + 1) * BS, :] = gather_ref[:, b * BS:(b + 1) * BS].astype(F32).T.astype(BF16)


def coarse_product(coarse2_ref, far_ref, own_ref, near_ref, window):
    rim, rows = far_ref.shape[0], own_ref.shape[0]
    odd = odd_tile()
    window[pl.ds(pl.multiple_of(odd * (rim + rows), 64), rim), :] = pair(far_ref[...])
    window[pl.ds(pl.multiple_of((1 - odd) * (rim + rows), 64), rim), :] = pair(near_ref[...])
    window[rim:rim + rows, :] = pair(own_ref[...])
    return folded_twice(dot(coarse2_ref[...], window[...]))


def advance(coarse2_ref, far_ref, own_ref, near_ref, jump_ref, later_ref, *refs):
    state_ref, nfar_ref, nnear_ref, total_ref, window = refs[-5:]
    image = coarse_product(coarse2_ref, far_ref, own_ref, near_ref, window)
    state_ref[...] = image + (jump_ref[...] - later_ref[...])
    sides(state_ref, nfar_ref, nnear_ref, nfar_ref.shape[0])
    total_ref[...] = image if len(refs) == 5 else refs[0][...] + image


def finish(coarse2_ref, far_ref, own_ref, near_ref, image_ref, spread_ref, end_ref, out_hbm, window, held, sems):
    image = image_ref[...] + coarse_product(coarse2_ref, far_ref, own_ref, near_ref, window)
    split = pair(image)
    copies = []
    for b in range(sems.shape[0]):
        part = end_ref.shape[0] // sems.shape[0]
        rows = slice(b * part, (b + 1) * part)
        held[rows, :] = end_ref[rows, :] + folded(dot(spread_ref[rows, :], split))
        copies.append(pltpu.make_async_copy(held.at[rows, :], out_hbm.at[rows, :], sems.at[b]))
        copies[-1].start()
    for copy in copies:
        copy.wait()


def swapped(far, near):
    count = lax.axis_size("tile")
    far = lax.ppermute(far, "tile", [(i, (i + 1 if i % 2 else i - 1) % count) for i in range(count)])
    near = lax.ppermute(near, "tile", [(i, i ^ 1) for i in range(count)])
    return far, near


def on_device(starts, sources, fine_ops, col_index, live_count, coarse_op, cell_map):
    first_state = starts[0]
    ops = fine_ops[0]
    rows, tracers = first_state.shape
    blocks, slots = ops.shape[:2]
    columns = col_index[0].T
    live = live_count
    coarse, reach = coarse_op.shape
    rim = (reach - coarse) // 2
    slices = lax.axis_size("tm")
    tiles = lax.axis_size("tile")
    window = pltpu.VMEM((rows + 2 * HALO, 2 * tracers), BF16)
    step_flops = 6 * rows * slots * BS * tracers
    coarse_flops = 6 * coarse * reach * tracers
    side = ((HALO, tracers), F32)
    coarse_rim = ((rim, tracers), F32)
    coarse_all = ((coarse, tracers), F32)

    far, near = call(ends, [side, side], [HBM], 0, 500_000, [pltpu.SemaphoreType.DMA((2,))])(kept(first_state))
    far, near = swapped(far, near)
    ops, own, sources = call(
        fetch, [(ops.shape, F32), ((rows, 2 * tracers), BF16), (sources.shape, F32)],
        [HBM] * 3, 0, 9_000_000, [pltpu.VMEM((rows, tracers), F32), pltpu.SemaphoreType.DMA((3,))],
    )(kept(ops), kept(first_state), kept(sources))

    step_in = [HBM] * 2 + [VMEM] * 5
    step_scratch = [pltpu.SMEM(columns.shape, jnp.int32), pltpu.SMEM(live.shape, jnp.int32), window,
                    pltpu.SemaphoreType.DMA((2,))]
    state, far, near, token = call(
        first_step, [((rows, 2 * tracers), BF16), side, side, ((8, tracers), F32)],
        step_in, step_flops, 6_000_000, step_scratch + [pltpu.VMEM((2 * HALO, tracers), F32)],
    )(kept(columns), kept(live), ops, own, far, near, sources)
    far, near = swapped(far, near)
    gather, inverse, rstart = call(
        prepare, [((coarse, rows), BF16), coarse_all, coarse_all],
        [HBM, VMEM, VMEM], 4 * coarse * rows * tracers, 3_000_000,
        [pltpu.VMEM((blocks, BS), jnp.int32), pltpu.SemaphoreType.DMA((1,))],
    )(kept(cell_map.reshape(-1, BS)), own, token)
    later = lax.ppermute(rstart, "tm", [(i + 1, i) for i in range(1, slices - 1)])
    following = lax.ppermute(rstart, "tm", [(1, 0)])
    step_scratch = step_scratch + [pltpu.VMEM((rows, 2 * tracers), BF16)]
    step_args = (kept(columns), kept(live), ops, state, far, near, sources, gather, inverse)
    step_flops = step_flops + 4 * coarse * rows * tracers
    fine_end, jump, far, near = call(
        second_step_first, [((rows, tracers), F32), coarse_all, coarse_rim, coarse_rim],
        step_in + [VMEM] * 3, step_flops, 8_000_000, step_scratch,
    )(*step_args, following)

    def to_slice(block, n, target):
        route = [((n - 1) * tiles + i, n * tiles + target(i) % tiles) for i in range(tiles)]
        return lax.ppermute(block, ("tm", "tile"), route)

    image = ()
    state = jump
    coarse_window = [pltpu.VMEM((reach, 2 * tracers), BF16)]
    for n in range(1, slices):
        far = to_slice(far, n, lambda i: i + 1 if i % 2 else i - 1)
        near = to_slice(near, n, lambda i: i ^ 1)
        own = to_slice(state, n, lambda i: i)
        if n == 1:
            fine_end, jump = call(
                second_step_one, [((rows, tracers), F32), coarse_all],
                step_in + [VMEM] * 3, step_flops, 8_000_000, step_scratch, aliases={9: 0},
            )(*step_args, fine_end)
            (coarse2,) = call(
                split_coarse, [((2 * coarse, reach), BF16)], [HBM, VMEM], 0, 4_000_000,
                [pltpu.VMEM((coarse, reach), F32), pltpu.SemaphoreType.DMA((1,))],
            )(kept(coarse_op), token)
        if n == 2:
            fine_end, jump, spread = call(
                second_step_others, [((rows, tracers), F32), coarse_all, ((rows, coarse), BF16)],
                step_in + [VMEM] * 3, step_flops, 8_000_000, step_scratch, aliases={9: 0},
            )(*step_args, fine_end)
        if n < slices - 1:
            state, far, near, *image = call(
                advance, [coarse_all, coarse_rim, coarse_rim, coarse_all],
                [VMEM] * (6 + len(image)), coarse_flops, 2_000_000, coarse_window,
            )(coarse2, far, own, near, jump, later, *image)
        else:
            (result,) = call(
                finish, [((rows, tracers), F32)], [VMEM] * 7,
                coarse_flops + 4 * coarse * rows * tracers, 4_000_000,
                coarse_window + [pltpu.VMEM((rows, tracers), F32), pltpu.SemaphoreType.DMA((6,))], HBM,
            )(coarse2, far, own, near, *image, spread, fine_end)
    return result[None]


def solution(mesh):
    placed = (
        P("tm", "tile", None),
        P("tile", None),
        P("tm", "tile", None, None, None),
        P("tm", "tile", None),
        P("tm", "tile"),
        P("tile", None),
        P("tile"),
    )

    return jax.shard_map(on_device, mesh=mesh, in_specs=placed, out_specs=P("tm", "tile", None), check_vma=False)
```

```python
import jax
import jax.numpy as jnp
from jax import lax
from jax.experimental import pallas as pl
from jax.experimental.pallas import tpu as pltpu
from jax.sharding import PartitionSpec as P


HALO = 256
BS = 128
F32 = jnp.float32
BF16 = jnp.bfloat16
VMEM = pl.BlockSpec(memory_space=pltpu.VMEM)
SMEM = pl.BlockSpec(memory_space=pltpu.SMEM)
HBM = pl.BlockSpec(memory_space=pltpu.HBM)


def call(kernel, outs, in_specs, flops, nbytes, scratch=(), out_spec=VMEM, aliases=None):
    return pl.pallas_call(
        kernel,
        out_shape=[jax.ShapeDtypeStruct(shape, dtype) for shape, dtype in outs],
        in_specs=in_specs,
        out_specs=[out_spec] * len(outs),
        input_output_aliases=aliases or {},
        scratch_shapes=list(scratch),
        cost_estimate=pl.CostEstimate(flops=flops, bytes_accessed=nbytes, transcendentals=0),
        compiler_params=pltpu.CompilerParams(vmem_limit_bytes=16 << 20),
    )


def kept(value):
    return pltpu.with_memory_space_constraint(value, pltpu.HBM)


def halves(value):
    high = value.astype(BF16)
    return high, (value - high.astype(F32)).astype(BF16)


def pair(value):
    return jnp.concatenate(halves(value), axis=1)


def dot(a, b):
    return jnp.dot(a, b, preferred_element_type=F32)


def folded(product):
    width = product.shape[1] // 2
    return product[:, :width] + product[:, width:]


def folded_twice(product):
    half = folded(product)
    rows = half.shape[0] // 2
    return half[:rows] + half[rows:]


def odd_tile():
    return lax.rem(lax.axis_index("tile"), 2)


def ends(starts_ref, far_ref, near_ref, sems):
    last = starts_ref.shape[0] - HALO
    odd = odd_tile()
    copies = [
        pltpu.make_async_copy(
            starts_ref.at[pl.ds(pl.multiple_of(side * last, BS), HALO), :], out_ref, sems.at[index]
        )
        for index, (side, out_ref) in enumerate(((odd, far_ref), (1 - odd, near_ref)))
    ]
    for copy in copies:
        copy.start()
    for copy in copies:
        copy.wait()


def run_copies(copies):
    for copy in copies:
        copy.start()
    return copies


def in_turn(kernel, operand_count, outs, in_specs, flops, nbytes, scratch, operands, order):
    def predicated(core, skipped):
        def body(*refs):
            @pl.when(lax.rem(lax.axis_index("tm"), 2) == core)
            def _():
                kernel(*refs[:operand_count], *refs[operand_count + skipped:])

        return body

    count = len(outs)
    held = call(predicated(1, 0), outs, in_specs, flops, nbytes, scratch)(*operands)
    between = order()
    held = call(
        predicated(0, count), outs, in_specs + [VMEM] * count, flops, nbytes, scratch,
        aliases={operand_count + index: index for index in range(count)},
    )(*operands, *held)
    return held, between


def fetch(ops_ref, starts_ref, sources_ref, ops_out, own_ref, sources_out, held, sems):
    copies = run_copies([
        pltpu.make_async_copy(starts_ref, held, sems.at[0]),
        pltpu.make_async_copy(ops_ref, ops_out, sems.at[1]),
        pltpu.make_async_copy(sources_ref, sources_out, sems.at[2]),
    ])
    copies[0].wait()
    for b in range(held.shape[0] // BS):
        own_ref[b * BS:(b + 1) * BS, :] = pair(held[b * BS:(b + 1) * BS, :])
    for copy in copies[1:]:
        copy.wait()


def prepare(map_hbm, own_ref, token_ref, gather_ref, inverse_ref, rstart_ref, map_ref, sems):
    copy = pltpu.make_async_copy(map_hbm, map_ref, sems.at[0])
    copy.start()
    copy.wait()
    coarse = gather_ref.shape[0]
    cells = lax.broadcasted_iota(jnp.int32, (coarse, BS), 0)
    children = jnp.zeros((coarse, 1), F32)
    for b in range(map_ref.shape[0]):
        chosen = jnp.where(map_ref[b:b + 1, :] == cells, 1.0, 0.0)
        children = children + jnp.sum(chosen, axis=1, keepdims=True)
        gather_ref[:, b * BS:(b + 1) * BS] = chosen.astype(BF16)
    inverse = jnp.broadcast_to(1.0 / children, inverse_ref.shape)
    inverse_ref[...] = inverse
    rstart_ref[...] = folded(dot(gather_ref[...], own_ref[...])) * inverse


def split_coarse(coarse_hbm, token_ref, coarse2_ref, coarse_ref, sems):
    copy = pltpu.make_async_copy(coarse_hbm, coarse_ref, sems.at[0])
    copy.start()
    copy.wait()
    rows = coarse_ref.shape[0]
    high, low = halves(coarse_ref[...])
    coarse2_ref[:rows, :] = high
    coarse2_ref[rows:, :] = low


def transport(cols_hbm, live_hbm, ops_ref, own_ref, far_ref, near_ref, sources_ref,
              cols_ref, live_ref, window, sems, emit):
    copies = run_copies([
        pltpu.make_async_copy(cols_hbm, cols_ref, sems.at[0]),
        pltpu.make_async_copy(live_hbm, live_ref, sems.at[1]),
    ])
    rows = own_ref.shape[0]
    blocks, slots = ops_ref.shape[:2]
    odd = odd_tile()
    window[pl.ds(pl.multiple_of(odd * (HALO + rows), BS), HALO), :] = pair(far_ref[...])
    window[pl.ds(pl.multiple_of((1 - odd) * (HALO + rows), BS), HALO), :] = pair(near_ref[...])
    window[HALO:HALO + rows, :] = own_ref[...]
    for copy in copies:
        copy.wait()
    for b in range(blocks):
        pieces, highs, lows = [], [], []
        for k in range(slots):
            at = pl.multiple_of(cols_ref[k, b] * BS, BS)
            pieces.append(window[pl.ds(at, BS), :])
            high, low = halves(jnp.where(k < live_ref[0, b], ops_ref[b, k], 0.0))
            highs.append(high)
            lows.append(low)
        pieces = jnp.concatenate(pieces, axis=0)
        operator = jnp.concatenate([jnp.concatenate(highs, axis=1), jnp.concatenate(lows, axis=1)], axis=0)
        value = folded_twice(dot(operator, pieces))
        emit(b, value + sources_ref[b * BS:(b + 1) * BS, :])


def sides(block, far_ref, near_ref, width):
    odd = odd_tile()
    last = block.shape[0] - width
    far_ref[...] = block[pl.ds(pl.multiple_of(odd * last, 64), width), :]
    near_ref[...] = block[pl.ds(pl.multiple_of((1 - odd) * last, 64), width), :]


def first_step(cols_hbm, live_hbm, ops_ref, own_ref, far_ref, near_ref, sources_ref,
               next_ref, nfar_ref, nnear_ref, token_ref, cols_ref, live_ref, window, sems, rims):
    blocks = ops_ref.shape[0]
    side = HALO // BS

    def emit(b, value):
        next_ref[b * BS:(b + 1) * BS, :] = pair(value)
        if b < side:
            rims[b * BS:(b + 1) * BS, :] = value
        if b >= blocks - side:
            at = b - blocks + 2 * side
            rims[at * BS:(at + 1) * BS, :] = value

    transport(cols_hbm, live_hbm, ops_ref, own_ref, far_ref, near_ref, sources_ref,
              cols_ref, live_ref, window, sems, emit)
    sides(rims, nfar_ref, nnear_ref, HALO)
    token_ref[...] = jnp.zeros_like(token_ref)


def restricted_step(refs, gather_ref, inverse_ref, end_ref, jump_ref, cols_ref, live_ref, window, sems, split):
    def emit(b, value):
        end_ref[b * BS:(b + 1) * BS, :] = value
        split[b * BS:(b + 1) * BS, :] = pair(value)

    transport(*refs, cols_ref, live_ref, window, sems, emit)
    jump_ref[...] = folded(dot(gather_ref[...], split[...])) * inverse_ref[...]


def second_step_first(*refs):
    operands, (gather_ref, inverse_ref, following_ref) = refs[:7], refs[7:10]
    end_ref, jump_ref, nfar_ref, nnear_ref = refs[10:14]

    @pl.when(lax.axis_index("tm") == 0)
    def _():
        restricted_step(operands, gather_ref, inverse_ref, end_ref, jump_ref, *refs[14:])
        jump_ref[...] = jump_ref[...] - following_ref[...]
        sides(jump_ref, nfar_ref, nnear_ref, nfar_ref.shape[0])


def second_step_rest(chosen, gather_ref, inverse_ref, operands, end_ref, jump_ref, scratch):
    @pl.when(jnp.logical_not(chosen))
    def _():
        jump_ref[...] = jnp.zeros_like(jump_ref)

    @pl.when(chosen)
    def _():
        restricted_step(operands, gather_ref, inverse_ref, end_ref, jump_ref, *scratch)


def second_step_one(*refs):
    second_step_rest(lax.axis_index("tm") == 1, refs[7], refs[8], refs[:7], refs[10], refs[11], refs[12:])


def second_step_others(*refs):
    second_step_rest(lax.axis_index("tm") > 1, refs[7], refs[8], refs[:7], refs[10], refs[11], refs[13:])
    gather_ref, spread_ref = refs[7], refs[12]
    for b in range(gather_ref.shape[1] // BS):
        spread_ref[b * BS:(b + 1) * BS, :] = gather_ref[:, b * BS:(b + 1) * BS].astype(F32).T.astype(BF16)


def fill(far_ref, own_ref, near_ref, window):
    rim, rows = far_ref.shape[0], own_ref.shape[0]
    odd = odd_tile()
    window[pl.ds(pl.multiple_of(odd * (rim + rows), 64), rim), :] = pair(far_ref[...])
    window[pl.ds(pl.multiple_of((1 - odd) * (rim + rows), 64), rim), :] = pair(near_ref[...])
    window[rim:rim + rows, :] = pair(own_ref[...])


def coarse_product(coarse2_ref, far_ref, own_ref, near_ref, window):
    fill(far_ref, own_ref, near_ref, window)
    return folded_twice(dot(coarse2_ref[...], window[...]))


def advance(coarse2_ref, far_ref, own_ref, near_ref, jump_ref, later_ref, *refs):
    state_ref, nfar_ref, nnear_ref, total_ref, window = refs[-5:]
    image = coarse_product(coarse2_ref, far_ref, own_ref, near_ref, window)
    state_ref[...] = image + (jump_ref[...] - later_ref[...])
    sides(state_ref, nfar_ref, nnear_ref, nfar_ref.shape[0])
    total_ref[...] = image if len(refs) == 5 else refs[0][...] + image


def finish(coarse2_ref, far_ref, own_ref, near_ref, image_ref, spread_ref, end_ref, out_hbm, window, held, sems):
    fill(far_ref, own_ref, near_ref, window)
    rows, tracers = own_ref.shape
    image = folded(dot(coarse2_ref[:rows, :], window[...]))
    image = image_ref[...] + image + dot(coarse2_ref[rows:, :], window[:, :tracers])
    split = pair(image)
    copies = []
    for b in range(sems.shape[0]):
        part = end_ref.shape[0] // sems.shape[0]
        rows = slice(b * part, (b + 1) * part)
        held[rows, :] = end_ref[rows, :] + folded(dot(spread_ref[rows, :], split))
        copies.append(pltpu.make_async_copy(held.at[rows, :], out_hbm.at[rows, :], sems.at[b]))
        copies[-1].start()
    for copy in copies:
        copy.wait()


def swapped(far, near):
    count = lax.axis_size("tile")
    far = lax.ppermute(far, "tile", [(i, (i + 1 if i % 2 else i - 1) % count) for i in range(count)])
    near = lax.ppermute(near, "tile", [(i, i ^ 1) for i in range(count)])
    return far, near


def on_device(starts, sources, fine_ops, col_index, live_count, coarse_op, cell_map):
    first_state = starts[0]
    ops = fine_ops[0]
    rows, tracers = first_state.shape
    blocks, slots = ops.shape[:2]
    columns = col_index[0].T
    live = live_count
    coarse, reach = coarse_op.shape
    rim = (reach - coarse) // 2
    slices = lax.axis_size("tm")
    tiles = lax.axis_size("tile")
    window = pltpu.VMEM((rows + 2 * HALO, 2 * tracers), BF16)
    step_flops = 6 * rows * slots * BS * tracers
    coarse_flops = 6 * coarse * reach * tracers
    side = ((HALO, tracers), F32)
    coarse_rim = ((rim, tracers), F32)
    coarse_all = ((coarse, tracers), F32)

    far, near = call(ends, [side, side], [HBM], 0, 500_000, [pltpu.SemaphoreType.DMA((2,))])(kept(first_state))
    (ops, own, sources), (far, near) = in_turn(
        fetch, 3, [(ops.shape, F32), ((rows, 2 * tracers), BF16), (sources.shape, F32)],
        [HBM] * 3, 0, 9_000_000, [pltpu.VMEM((rows, tracers), F32), pltpu.SemaphoreType.DMA((3,))],
        (kept(ops), kept(first_state), kept(sources)), lambda: swapped(far, near),
    )

    step_in = [HBM] * 2 + [VMEM] * 5
    step_scratch = [pltpu.SMEM(columns.shape, jnp.int32), pltpu.SMEM(live.shape, jnp.int32), window,
                    pltpu.SemaphoreType.DMA((2,))]
    state, far, near, token = call(
        first_step, [((rows, 2 * tracers), BF16), side, side, ((8, tracers), F32)],
        step_in, step_flops, 6_000_000, step_scratch + [pltpu.VMEM((2 * HALO, tracers), F32)],
    )(kept(columns), kept(live), ops, own, far, near, sources)
    (gather, inverse, rstart), (far, near) = in_turn(
        prepare, 3, [((coarse, rows), BF16), coarse_all, coarse_all],
        [HBM, VMEM, VMEM], 4 * coarse * rows * tracers, 3_000_000,
        [pltpu.VMEM((blocks, BS), jnp.int32), pltpu.SemaphoreType.DMA((1,))],
        (kept(cell_map.reshape(-1, BS)), own, token), lambda: swapped(far, near),
    )
    later = lax.ppermute(rstart, "tm", [(i + 1, i) for i in range(1, slices - 1)])
    following = lax.ppermute(rstart, "tm", [(1, 0)])
    step_scratch = step_scratch + [pltpu.VMEM((rows, 2 * tracers), BF16)]
    step_args = (kept(columns), kept(live), ops, state, far, near, sources, gather, inverse)
    step_flops = step_flops + 4 * coarse * rows * tracers
    fine_end, jump, far, near = call(
        second_step_first, [((rows, tracers), F32), coarse_all, coarse_rim, coarse_rim],
        step_in + [VMEM] * 3, step_flops, 8_000_000, step_scratch,
    )(*step_args, following)

    def to_slice(block, n, target):
        route = [((n - 1) * tiles + i, n * tiles + target(i) % tiles) for i in range(tiles)]
        return lax.ppermute(block, ("tm", "tile"), route)

    image = ()
    state = jump
    coarse_window = [pltpu.VMEM((reach, 2 * tracers), BF16)]
    for n in range(1, slices):
        far = to_slice(far, n, lambda i: i + 1 if i % 2 else i - 1)
        near = to_slice(near, n, lambda i: i ^ 1)
        own = to_slice(state, n, lambda i: i)
        if n == 1:
            fine_end, jump = call(
                second_step_one, [((rows, tracers), F32), coarse_all],
                step_in + [VMEM] * 3, step_flops, 8_000_000, step_scratch, aliases={9: 0},
            )(*step_args, fine_end)
            (coarse2,) = call(
                split_coarse, [((2 * coarse, reach), BF16)], [HBM, VMEM], 0, 4_000_000,
                [pltpu.VMEM((coarse, reach), F32), pltpu.SemaphoreType.DMA((1,))],
            )(kept(coarse_op), token)
        if n == 2:
            fine_end, jump, spread = call(
                second_step_others, [((rows, tracers), F32), coarse_all, ((rows, coarse), BF16)],
                step_in + [VMEM] * 3, step_flops, 8_000_000, step_scratch, aliases={9: 0},
            )(*step_args, fine_end)
        if n < slices - 1:
            state, far, near, *image = call(
                advance, [coarse_all, coarse_rim, coarse_rim, coarse_all],
                [VMEM] * (6 + len(image)), coarse_flops, 2_000_000, coarse_window,
            )(coarse2, far, own, near, jump, later, *image)
        else:
            (result,) = call(
                finish, [((rows, tracers), F32)], [VMEM] * 7,
                coarse_flops + 4 * coarse * rows * tracers, 4_000_000,
                coarse_window + [pltpu.VMEM((rows, tracers), F32), pltpu.SemaphoreType.DMA((6,))], HBM,
            )(coarse2, far, own, near, *image, spread, fine_end)
    return result[None]


def solution(mesh):
    placed = (
        P("tm", "tile", None),
        P("tile", None),
        P("tm", "tile", None, None, None),
        P("tm", "tile", None),
        P("tm", "tile"),
        P("tile", None),
        P("tile"),
    )

    return jax.shard_map(on_device, mesh=mesh, in_specs=placed, out_specs=P("tm", "tile", None), check_vma=False)
```

```python
import jax
import jax.numpy as jnp
from jax import lax
from jax.experimental import pallas as pl
from jax.experimental.pallas import tpu as pltpu
from jax.sharding import PartitionSpec as P


HALO = 256
PLANE = 16
BS = 128
F32 = jnp.float32
BF16 = jnp.bfloat16
VMEM = pl.BlockSpec(memory_space=pltpu.VMEM)
SMEM = pl.BlockSpec(memory_space=pltpu.SMEM)
HBM = pl.BlockSpec(memory_space=pltpu.HBM)


def call(kernel, outs, in_specs, flops, nbytes, scratch=(), out_spec=VMEM, aliases=None):
    return pl.pallas_call(
        kernel,
        out_shape=[jax.ShapeDtypeStruct(shape, dtype) for shape, dtype in outs],
        in_specs=in_specs,
        out_specs=[out_spec] * len(outs),
        input_output_aliases=aliases or {},
        scratch_shapes=list(scratch),
        cost_estimate=pl.CostEstimate(flops=flops, bytes_accessed=nbytes, transcendentals=0),
        compiler_params=pltpu.CompilerParams(vmem_limit_bytes=16 << 20),
    )


def kept(value):
    return pltpu.with_memory_space_constraint(value, pltpu.HBM)


def halves(value):
    high = value.astype(BF16)
    return high, (value - high.astype(F32)).astype(BF16)


def pair(value):
    return jnp.concatenate(halves(value), axis=1)


def dot(a, b):
    return jnp.dot(a, b, preferred_element_type=F32)


def folded(product):
    width = product.shape[1] // 2
    return product[:, :width] + product[:, width:]


def folded_twice(product):
    half = folded(product)
    rows = half.shape[0] // 2
    return half[:rows] + half[rows:]


def odd_tile():
    return lax.rem(lax.axis_index("tile"), 2)


def ends(starts_ref, far_ref, near_ref, sems):
    last = starts_ref.shape[0] - HALO
    odd = odd_tile()
    copies = [
        pltpu.make_async_copy(
            starts_ref.at[pl.ds(pl.multiple_of(side * last, BS), HALO), :], out_ref, sems.at[index]
        )
        for index, (side, out_ref) in enumerate(((odd, far_ref), (1 - odd, near_ref)))
    ]
    for copy in copies:
        copy.start()
    for copy in copies:
        copy.wait()


def run_copies(copies):
    for copy in copies:
        copy.start()
    return copies


def fetch(ops_ref, starts_ref, sources_ref, ops_out, own_ref, sources_out, held, sems):
    copies = run_copies([
        pltpu.make_async_copy(starts_ref, held, sems.at[0]),
        pltpu.make_async_copy(ops_ref, ops_out, sems.at[1]),
        pltpu.make_async_copy(sources_ref, sources_out, sems.at[2]),
    ])
    copies[0].wait()
    for b in range(held.shape[0] // BS):
        own_ref[b * BS:(b + 1) * BS, :] = pair(held[b * BS:(b + 1) * BS, :])
    for copy in copies[1:]:
        copy.wait()


def prepare(map_hbm, own_ref, token_ref, gather_ref, inverse_ref, rstart_ref, map_ref, sems):
    copy = pltpu.make_async_copy(map_hbm, map_ref, sems.at[0])
    copy.start()
    copy.wait()
    coarse = gather_ref.shape[0]
    cells = lax.broadcasted_iota(jnp.int32, (coarse, BS), 0)
    children = jnp.zeros((coarse, 1), F32)
    for b in range(map_ref.shape[0]):
        chosen = jnp.where(map_ref[b:b + 1, :] == cells, 1.0, 0.0)
        children = children + jnp.sum(chosen, axis=1, keepdims=True)
        gather_ref[:, b * BS:(b + 1) * BS] = chosen.astype(BF16)
    inverse = jnp.broadcast_to(1.0 / children, inverse_ref.shape)
    inverse_ref[...] = inverse
    rstart_ref[...] = folded(dot(gather_ref[...], own_ref[...])) * inverse


def split_coarse(coarse_hbm, token_ref, coarse2_ref, coarse_ref, sems):
    copy = pltpu.make_async_copy(coarse_hbm, coarse_ref, sems.at[0])
    copy.start()
    copy.wait()
    rows = coarse_ref.shape[0]
    high, low = halves(coarse_ref[...])
    coarse2_ref[:rows, :] = high
    coarse2_ref[rows:, :] = low


def transport(cols_hbm, live_hbm, ops_ref, own_ref, far_ref, near_ref, sources_ref,
              cols_ref, live_ref, window, sems, emit):
    copies = run_copies([
        pltpu.make_async_copy(cols_hbm, cols_ref, sems.at[0]),
        pltpu.make_async_copy(live_hbm, live_ref, sems.at[1]),
    ])
    rows = own_ref.shape[0]
    blocks, slots = ops_ref.shape[:2]
    odd = odd_tile()
    window[pl.ds(pl.multiple_of(odd * (HALO + rows), BS), HALO), :] = pair(far_ref[...])
    window[pl.ds(pl.multiple_of((1 - odd) * (HALO + rows), BS), HALO), :] = pair(near_ref[...])
    window[HALO:HALO + rows, :] = own_ref[...]
    for copy in copies:
        copy.wait()
    for b in range(blocks):
        pieces, highs, lows = [], [], []
        for k in range(slots):
            at = pl.multiple_of(cols_ref[k, b] * BS, BS)
            pieces.append(window[pl.ds(at, BS), :])
            high, low = halves(jnp.where(k < live_ref[0, b], ops_ref[b, k], 0.0))
            highs.append(high)
            lows.append(low)
        pieces = jnp.concatenate(pieces, axis=0)
        operator = jnp.concatenate([jnp.concatenate(highs, axis=1), jnp.concatenate(lows, axis=1)], axis=0)
        value = folded_twice(dot(operator, pieces))
        emit(b, value + sources_ref[b * BS:(b + 1) * BS, :])


def sides(block, far_ref, near_ref, width):
    odd = odd_tile()
    last = block.shape[0] - width
    far_ref[...] = block[pl.ds(pl.multiple_of(odd * last, 64), width), :]
    near_ref[...] = block[pl.ds(pl.multiple_of((1 - odd) * last, 64), width), :]


def first_step(cols_hbm, live_hbm, ops_ref, own_ref, far_ref, near_ref, sources_ref, last_ref,
               next_ref, nfar_ref, nnear_ref, token_ref, cols_ref, live_ref, window, sems, rims, whole):
    blocks = ops_ref.shape[0]
    side = HALO // BS

    def emit(b, value):
        next_ref[b * BS:(b + 1) * BS, :] = pair(value)
        if b < side:
            rims[b * BS:(b + 1) * BS, :] = value
        if b >= blocks - side:
            at = b - blocks + 2 * side
            rims[at * BS:(at + 1) * BS, :] = value

    whole[...] = near_ref[...] + last_ref[...]
    transport(cols_hbm, live_hbm, ops_ref, own_ref, far_ref, whole, sources_ref,
              cols_ref, live_ref, window, sems, emit)
    sides(rims, nfar_ref, nnear_ref, HALO)
    token_ref[...] = jnp.zeros_like(token_ref)


def restricted_step(refs, gather_ref, inverse_ref, end_ref, jump_ref, cols_ref, live_ref, window, sems, split):
    def emit(b, value):
        end_ref[b * BS:(b + 1) * BS, :] = value
        split[b * BS:(b + 1) * BS, :] = pair(value)

    transport(*refs, cols_ref, live_ref, window, sems, emit)
    jump_ref[...] = folded(dot(gather_ref[...], split[...])) * inverse_ref[...]


def second_step_first(*refs):
    operands, (gather_ref, inverse_ref, following_ref) = refs[:7], refs[7:10]
    end_ref, jump_ref, nfar_ref, nnear_ref = refs[10:14]

    @pl.when(lax.axis_index("tm") == 0)
    def _():
        restricted_step(operands, gather_ref, inverse_ref, end_ref, jump_ref, *refs[14:])
        jump_ref[...] = jump_ref[...] - following_ref[...]
        sides(jump_ref, nfar_ref, nnear_ref, nfar_ref.shape[0])


def second_step_rest(chosen, gather_ref, inverse_ref, operands, end_ref, jump_ref, scratch):
    @pl.when(jnp.logical_not(chosen))
    def _():
        jump_ref[...] = jnp.zeros_like(jump_ref)

    @pl.when(chosen)
    def _():
        restricted_step(operands, gather_ref, inverse_ref, end_ref, jump_ref, *scratch)


def second_step_one(*refs):
    second_step_rest(lax.axis_index("tm") == 1, refs[7], refs[8], refs[:7], refs[10], refs[11], refs[12:])


def second_step_others(*refs):
    second_step_rest(lax.axis_index("tm") > 1, refs[7], refs[8], refs[:7], refs[10], refs[11], refs[13:])
    gather_ref, spread_ref = refs[7], refs[12]
    for b in range(gather_ref.shape[1] // BS):
        spread_ref[b * BS:(b + 1) * BS, :] = gather_ref[:, b * BS:(b + 1) * BS].astype(F32).T.astype(BF16)


def fill(far_ref, own_ref, near_ref, window):
    rim, rows = far_ref.shape[0], own_ref.shape[0]
    odd = odd_tile()
    window[pl.ds(pl.multiple_of(odd * (rim + rows), 64), rim), :] = pair(far_ref[...])
    window[pl.ds(pl.multiple_of((1 - odd) * (rim + rows), 64), rim), :] = pair(near_ref[...])
    window[rim:rim + rows, :] = pair(own_ref[...])


def coarse_product(coarse2_ref, far_ref, own_ref, near_ref, window):
    fill(far_ref, own_ref, near_ref, window)
    return folded_twice(dot(coarse2_ref[...], window[...]))


def advance(coarse2_ref, far_ref, own_ref, near_ref, jump_ref, later_ref, *refs):
    state_ref, nfar_ref, nnear_ref, total_ref, window = refs[-5:]
    image = coarse_product(coarse2_ref, far_ref, own_ref, near_ref, window)
    state_ref[...] = image + (jump_ref[...] - later_ref[...])
    sides(state_ref, nfar_ref, nnear_ref, nfar_ref.shape[0])
    total_ref[...] = image if len(refs) == 5 else refs[0][...] + image


def finish(coarse2_ref, far_ref, own_ref, near_ref, image_ref, spread_ref, end_ref, out_hbm, window, held, sems):
    fill(far_ref, own_ref, near_ref, window)
    rows, tracers = own_ref.shape
    image = folded(dot(coarse2_ref[:rows, :], window[...]))
    image = image_ref[...] + image + dot(coarse2_ref[rows:, :], window[:, :tracers])
    split = pair(image)
    copies = []
    for b in range(sems.shape[0]):
        part = end_ref.shape[0] // sems.shape[0]
        rows = slice(b * part, (b + 1) * part)
        held[rows, :] = end_ref[rows, :] + folded(dot(spread_ref[rows, :], split))
        copies.append(pltpu.make_async_copy(held.at[rows, :], out_hbm.at[rows, :], sems.at[b]))
        copies[-1].start()
    for copy in copies:
        copy.wait()


def swapped(far, near):
    count = lax.axis_size("tile")
    far = lax.ppermute(far, "tile", [(i, (i + 1 if i % 2 else i - 1) % count) for i in range(count)])
    near = lax.ppermute(near, "tile", [(i, i ^ 1) for i in range(count)])
    return far, near


def swapped_early(far, near):
    count = lax.axis_size("tile")
    last = [i for i in range(count) if i % PLANE >= PLANE - 2]
    first = lax.ppermute(near, "tile", [(i, i ^ 1) for i in range(count) if i not in last])
    far = lax.ppermute(far, "tile", [(i, (i + 1 if i % 2 else i - 1) % count) for i in range(count)])
    second = lax.ppermute(near, "tile", [(i, i ^ 1) for i in last])
    return far, first, second


def on_device(starts, sources, fine_ops, col_index, live_count, coarse_op, cell_map):
    first_state = starts[0]
    ops = fine_ops[0]
    rows, tracers = first_state.shape
    blocks, slots = ops.shape[:2]
    columns = col_index[0].T
    live = live_count
    coarse, reach = coarse_op.shape
    rim = (reach - coarse) // 2
    slices = lax.axis_size("tm")
    tiles = lax.axis_size("tile")
    window = pltpu.VMEM((rows + 2 * HALO, 2 * tracers), BF16)
    step_flops = 6 * rows * slots * BS * tracers
    coarse_flops = 6 * coarse * reach * tracers
    side = ((HALO, tracers), F32)
    coarse_rim = ((rim, tracers), F32)
    coarse_all = ((coarse, tracers), F32)

    far, near = call(ends, [side, side], [HBM], 0, 500_000, [pltpu.SemaphoreType.DMA((2,))])(kept(first_state))
    far, near, last = swapped_early(far, near)
    ops, own, sources = call(
        fetch, [(ops.shape, F32), ((rows, 2 * tracers), BF16), (sources.shape, F32)],
        [HBM] * 3, 0, 9_000_000, [pltpu.VMEM((rows, tracers), F32), pltpu.SemaphoreType.DMA((3,))],
    )(kept(ops), kept(first_state), kept(sources))

    step_in = [HBM] * 2 + [VMEM] * 5
    step_scratch = [pltpu.SMEM(columns.shape, jnp.int32), pltpu.SMEM(live.shape, jnp.int32), window,
                    pltpu.SemaphoreType.DMA((2,))]
    state, far, near, token = call(
        first_step, [((rows, 2 * tracers), BF16), side, side, ((8, tracers), F32)],
        step_in + [VMEM], step_flops, 6_000_000,
        step_scratch + [pltpu.VMEM((2 * HALO, tracers), F32), pltpu.VMEM((HALO, tracers), F32)],
    )(kept(columns), kept(live), ops, own, far, near, sources, last)
    far, near = swapped(far, near)
    gather, inverse, rstart = call(
        prepare, [((coarse, rows), BF16), coarse_all, coarse_all],
        [HBM, VMEM, VMEM], 4 * coarse * rows * tracers, 3_000_000,
        [pltpu.VMEM((blocks, BS), jnp.int32), pltpu.SemaphoreType.DMA((1,))],
    )(kept(cell_map.reshape(-1, BS)), own, token)
    later = lax.ppermute(rstart, "tm", [(i + 1, i) for i in range(1, slices - 1)])
    following = lax.ppermute(rstart, "tm", [(1, 0)])
    step_scratch = step_scratch + [pltpu.VMEM((rows, 2 * tracers), BF16)]
    step_args = (kept(columns), kept(live), ops, state, far, near, sources, gather, inverse)
    step_flops = step_flops + 4 * coarse * rows * tracers
    fine_end, jump, far, near = call(
        second_step_first, [((rows, tracers), F32), coarse_all, coarse_rim, coarse_rim],
        step_in + [VMEM] * 3, step_flops, 8_000_000, step_scratch,
    )(*step_args, following)

    def to_slice(block, n, target):
        route = [((n - 1) * tiles + i, n * tiles + target(i) % tiles) for i in range(tiles)]
        return lax.ppermute(block, ("tm", "tile"), route)

    image = ()
    state = jump
    coarse_window = [pltpu.VMEM((reach, 2 * tracers), BF16)]
    for n in range(1, slices):
        far = to_slice(far, n, lambda i: i + 1 if i % 2 else i - 1)
        near = to_slice(near, n, lambda i: i ^ 1)
        own = to_slice(state, n, lambda i: i)
        if n == 1:
            fine_end, jump = call(
                second_step_one, [((rows, tracers), F32), coarse_all],
                step_in + [VMEM] * 3, step_flops, 8_000_000, step_scratch, aliases={9: 0},
            )(*step_args, fine_end)
            (coarse2,) = call(
                split_coarse, [((2 * coarse, reach), BF16)], [HBM, VMEM], 0, 4_000_000,
                [pltpu.VMEM((coarse, reach), F32), pltpu.SemaphoreType.DMA((1,))],
            )(kept(coarse_op), token)
        if n == 2:
            fine_end, jump, spread = call(
                second_step_others, [((rows, tracers), F32), coarse_all, ((rows, coarse), BF16)],
                step_in + [VMEM] * 3, step_flops, 8_000_000, step_scratch, aliases={9: 0},
            )(*step_args, fine_end)
        if n < slices - 1:
            state, far, near, *image = call(
                advance, [coarse_all, coarse_rim, coarse_rim, coarse_all],
                [VMEM] * (6 + len(image)), coarse_flops, 2_000_000, coarse_window,
            )(coarse2, far, own, near, jump, later, *image)
        else:
            (result,) = call(
                finish, [((rows, tracers), F32)], [VMEM] * 7,
                coarse_flops + 4 * coarse * rows * tracers, 4_000_000,
                coarse_window + [pltpu.VMEM((rows, tracers), F32), pltpu.SemaphoreType.DMA((6,))], HBM,
            )(coarse2, far, own, near, *image, spread, fine_end)
    return result[None]


def solution(mesh):
    placed = (
        P("tm", "tile", None),
        P("tile", None),
        P("tm", "tile", None, None, None),
        P("tm", "tile", None),
        P("tm", "tile"),
        P("tile", None),
        P("tile"),
    )

    return jax.shard_map(on_device, mesh=mesh, in_specs=placed, out_specs=P("tm", "tile", None), check_vma=False)
```

```python
import jax
import jax.numpy as jnp
from jax import lax
from jax.experimental import pallas as pl
from jax.experimental.pallas import tpu as pltpu
from jax.sharding import PartitionSpec as P


HALO = 256
PLANE = 16
BS = 128
F32 = jnp.float32
BF16 = jnp.bfloat16
VMEM = pl.BlockSpec(memory_space=pltpu.VMEM)
SMEM = pl.BlockSpec(memory_space=pltpu.SMEM)
HBM = pl.BlockSpec(memory_space=pltpu.HBM)


def call(kernel, outs, in_specs, flops, nbytes, scratch=(), out_spec=VMEM, aliases=None):
    return pl.pallas_call(
        kernel,
        out_shape=[jax.ShapeDtypeStruct(shape, dtype) for shape, dtype in outs],
        in_specs=in_specs,
        out_specs=[out_spec] * len(outs),
        input_output_aliases=aliases or {},
        scratch_shapes=list(scratch),
        cost_estimate=pl.CostEstimate(flops=flops, bytes_accessed=nbytes, transcendentals=0),
        compiler_params=pltpu.CompilerParams(vmem_limit_bytes=16 << 20),
    )


def kept(value):
    return pltpu.with_memory_space_constraint(value, pltpu.HBM)


def halves(value):
    high = value.astype(BF16)
    return high, (value - high.astype(F32)).astype(BF16)


def pair(value):
    return jnp.concatenate(halves(value), axis=1)


def dot(a, b):
    return jnp.dot(a, b, preferred_element_type=F32)


def folded(product):
    width = product.shape[1] // 2
    return product[:, :width] + product[:, width:]


def folded_twice(product):
    half = folded(product)
    rows = half.shape[0] // 2
    return half[:rows] + half[rows:]


def odd_tile():
    return lax.rem(lax.axis_index("tile"), 2)


def ends(starts_ref, far_ref, near_ref, sems):
    last = starts_ref.shape[0] - HALO
    odd = odd_tile()
    copies = [
        pltpu.make_async_copy(
            starts_ref.at[pl.ds(pl.multiple_of(side * last, BS), HALO), :], out_ref, sems.at[index]
        )
        for index, (side, out_ref) in enumerate(((odd, far_ref), (1 - odd, near_ref)))
    ]
    for copy in copies:
        copy.start()
    for copy in copies:
        copy.wait()


def run_copies(copies):
    for copy in copies:
        copy.start()
    return copies


def fetch(ops_ref, starts_ref, sources_ref, ops_out, own_ref, sources_out, held, sems):
    copies = run_copies([
        pltpu.make_async_copy(starts_ref, held, sems.at[0]),
        pltpu.make_async_copy(ops_ref, ops_out, sems.at[1]),
        pltpu.make_async_copy(sources_ref, sources_out, sems.at[2]),
    ])
    copies[0].wait()
    for b in range(held.shape[0] // BS):
        own_ref[b * BS:(b + 1) * BS, :] = pair(held[b * BS:(b + 1) * BS, :])
    for copy in copies[1:]:
        copy.wait()


def prepare(map_hbm, own_ref, token_ref, gather_ref, inverse_ref, rstart_ref, map_ref, sems):
    copy = pltpu.make_async_copy(map_hbm, map_ref, sems.at[0])
    copy.start()
    copy.wait()
    coarse = gather_ref.shape[0]
    cells = lax.broadcasted_iota(jnp.int32, (coarse, BS), 0)
    children = jnp.zeros((coarse, 1), F32)
    for b in range(map_ref.shape[0]):
        chosen = jnp.where(map_ref[b:b + 1, :] == cells, 1.0, 0.0)
        children = children + jnp.sum(chosen, axis=1, keepdims=True)
        gather_ref[:, b * BS:(b + 1) * BS] = chosen.astype(BF16)
    inverse = jnp.broadcast_to(1.0 / children, inverse_ref.shape)
    inverse_ref[...] = inverse
    rstart_ref[...] = folded(dot(gather_ref[...], own_ref[...])) * inverse


def split_coarse(coarse_hbm, token_ref, coarse2_ref, coarse_ref, sems):
    copy = pltpu.make_async_copy(coarse_hbm, coarse_ref, sems.at[0])
    copy.start()
    copy.wait()
    rows = coarse_ref.shape[0]
    high, low = halves(coarse_ref[...])
    coarse2_ref[:rows, :] = high
    coarse2_ref[rows:, :] = low


def transport(cols_hbm, live_hbm, ops_ref, own_ref, far_ref, near_ref, sources_ref,
              cols_ref, live_ref, window, sems, emit):
    copies = run_copies([
        pltpu.make_async_copy(cols_hbm, cols_ref, sems.at[0]),
        pltpu.make_async_copy(live_hbm, live_ref, sems.at[1]),
    ])
    rows = own_ref.shape[0]
    blocks, slots = ops_ref.shape[:2]
    odd = odd_tile()
    window[pl.ds(pl.multiple_of(odd * (HALO + rows), BS), HALO), :] = pair(far_ref[...])
    window[pl.ds(pl.multiple_of((1 - odd) * (HALO + rows), BS), HALO), :] = pair(near_ref[...])
    window[HALO:HALO + rows, :] = own_ref[...]
    for copy in copies:
        copy.wait()
    for b in range(blocks):
        pieces, highs, lows = [], [], []
        for k in range(slots):
            at = pl.multiple_of(cols_ref[k, b] * BS, BS)
            pieces.append(window[pl.ds(at, BS), :])
            high, low = halves(jnp.where(k < live_ref[0, b], ops_ref[b, k], 0.0))
            highs.append(high)
            lows.append(low)
        pieces = jnp.concatenate(pieces, axis=0)
        operator = jnp.concatenate([jnp.concatenate(highs, axis=1), jnp.concatenate(lows, axis=1)], axis=0)
        value = folded_twice(dot(operator, pieces))
        emit(b, value + sources_ref[b * BS:(b + 1) * BS, :])


def sides(block, far_ref, near_ref, width):
    odd = odd_tile()
    last = block.shape[0] - width
    far_ref[...] = block[pl.ds(pl.multiple_of(odd * last, 64), width), :]
    near_ref[...] = block[pl.ds(pl.multiple_of((1 - odd) * last, 64), width), :]


def first_step(cols_hbm, live_hbm, ops_ref, own_ref, far_ref, near_ref, sources_ref, last_ref,
               next_ref, nfar_ref, nnear_ref, cols_ref, live_ref, window, sems, rims, whole):
    blocks = ops_ref.shape[0]
    side = HALO // BS

    def emit(b, value):
        next_ref[b * BS:(b + 1) * BS, :] = pair(value)
        if b < side:
            rims[b * BS:(b + 1) * BS, :] = value
        if b >= blocks - side:
            at = b - blocks + 2 * side
            rims[at * BS:(at + 1) * BS, :] = value

    whole[...] = near_ref[...] + last_ref[...]
    transport(cols_hbm, live_hbm, ops_ref, own_ref, far_ref, whole, sources_ref,
              cols_ref, live_ref, window, sems, emit)
    sides(rims, nfar_ref, nnear_ref, HALO)


def late_tile():
    return lax.rem(lax.axis_index("tile"), PLANE) == PLANE - 1


def first_step_early(*refs):
    @pl.when(jnp.logical_not(late_tile()))
    def _():
        first_step(*refs)


def first_step_late(*refs):
    far_ref, near_ref = refs[9:11]
    nfar_ref, nnear_ref, token_ref = refs[12:15]
    token_ref[...] = jnp.zeros_like(token_ref)
    late = late_tile()

    @pl.when(jnp.logical_not(late))
    def _():
        nfar_ref[...] = far_ref[...]
        nnear_ref[...] = near_ref[...]

    @pl.when(late)
    def _():
        first_step(*refs[:8], *refs[11:14], *refs[15:])


def restricted_step(refs, gather_ref, inverse_ref, end_ref, jump_ref, cols_ref, live_ref, window, sems, split, whole):
    def emit(b, value):
        end_ref[b * BS:(b + 1) * BS, :] = value
        split[b * BS:(b + 1) * BS, :] = pair(value)

    whole[...] = refs[4][...] + refs[7][...]
    transport(*refs[:4], whole, *refs[5:7], cols_ref, live_ref, window, sems, emit)
    jump_ref[...] = folded(dot(gather_ref[...], split[...])) * inverse_ref[...]


def second_step_first(*refs):
    operands, (gather_ref, inverse_ref, following_ref) = refs[:8], refs[8:11]
    end_ref, jump_ref, nfar_ref, nnear_ref = refs[11:15]

    @pl.when(lax.axis_index("tm") == 0)
    def _():
        restricted_step(operands, gather_ref, inverse_ref, end_ref, jump_ref, *refs[15:])
        jump_ref[...] = jump_ref[...] - following_ref[...]
        sides(jump_ref, nfar_ref, nnear_ref, nfar_ref.shape[0])


def second_step_rest(chosen, gather_ref, inverse_ref, operands, end_ref, jump_ref, scratch):
    @pl.when(jnp.logical_not(chosen))
    def _():
        jump_ref[...] = jnp.zeros_like(jump_ref)

    @pl.when(chosen)
    def _():
        restricted_step(operands, gather_ref, inverse_ref, end_ref, jump_ref, *scratch)


def second_step_one(*refs):
    second_step_rest(lax.axis_index("tm") == 1, refs[8], refs[9], refs[:8], refs[11], refs[12], refs[13:])


def second_step_others(*refs):
    second_step_rest(lax.axis_index("tm") > 1, refs[8], refs[9], refs[:8], refs[11], refs[12], refs[14:])
    gather_ref, spread_ref = refs[8], refs[13]
    for b in range(gather_ref.shape[1] // BS):
        spread_ref[b * BS:(b + 1) * BS, :] = gather_ref[:, b * BS:(b + 1) * BS].astype(F32).T.astype(BF16)


def fill(far_ref, own_ref, near_ref, window):
    rim, rows = far_ref.shape[0], own_ref.shape[0]
    odd = odd_tile()
    window[pl.ds(pl.multiple_of(odd * (rim + rows), 64), rim), :] = pair(far_ref[...])
    window[pl.ds(pl.multiple_of((1 - odd) * (rim + rows), 64), rim), :] = pair(near_ref[...])
    window[rim:rim + rows, :] = pair(own_ref[...])


def coarse_product(coarse2_ref, far_ref, own_ref, near_ref, window):
    fill(far_ref, own_ref, near_ref, window)
    return folded_twice(dot(coarse2_ref[...], window[...]))


def advance(coarse2_ref, far_ref, own_ref, near_ref, jump_ref, later_ref, *refs):
    state_ref, nfar_ref, nnear_ref, total_ref, window = refs[-5:]
    image = coarse_product(coarse2_ref, far_ref, own_ref, near_ref, window)
    state_ref[...] = image + (jump_ref[...] - later_ref[...])
    sides(state_ref, nfar_ref, nnear_ref, nfar_ref.shape[0])
    total_ref[...] = image if len(refs) == 5 else refs[0][...] + image


def finish(coarse2_ref, far_ref, own_ref, near_ref, image_ref, spread_ref, end_ref, out_hbm, window, held, sems):
    fill(far_ref, own_ref, near_ref, window)
    rows, tracers = own_ref.shape
    image = folded(dot(coarse2_ref[:rows, :], window[...]))
    image = image_ref[...] + image + dot(coarse2_ref[rows:, :], window[:, :tracers])
    split = pair(image)
    copies = []
    for b in range(sems.shape[0]):
        part = end_ref.shape[0] // sems.shape[0]
        rows = slice(b * part, (b + 1) * part)
        held[rows, :] = end_ref[rows, :] + folded(dot(spread_ref[rows, :], split))
        copies.append(pltpu.make_async_copy(held.at[rows, :], out_hbm.at[rows, :], sems.at[b]))
        copies[-1].start()
    for copy in copies:
        copy.wait()


def swapped_first(far, near):
    count = lax.axis_size("tile")
    early = [i for i in range(count) if i % PLANE < 2]
    first = lax.ppermute(near, "tile", [(i, i ^ 1) for i in early])
    far = lax.ppermute(far, "tile", [(i, (i + 1 if i % 2 else i - 1) % count) for i in range(count)])
    second = lax.ppermute(near, "tile", [(i, i ^ 1) for i in range(count) if i not in early])
    return far, first, second


def on_device(starts, sources, fine_ops, col_index, live_count, coarse_op, cell_map):
    first_state = starts[0]
    ops = fine_ops[0]
    rows, tracers = first_state.shape
    blocks, slots = ops.shape[:2]
    columns = col_index[0].T
    live = live_count
    coarse, reach = coarse_op.shape
    rim = (reach - coarse) // 2
    slices = lax.axis_size("tm")
    tiles = lax.axis_size("tile")
    window = pltpu.VMEM((rows + 2 * HALO, 2 * tracers), BF16)
    step_flops = 6 * rows * slots * BS * tracers
    coarse_flops = 6 * coarse * reach * tracers
    side = ((HALO, tracers), F32)
    coarse_rim = ((rim, tracers), F32)
    coarse_all = ((coarse, tracers), F32)

    far, near = call(ends, [side, side], [HBM], 0, 500_000, [pltpu.SemaphoreType.DMA((2,))])(kept(first_state))
    far, near, last = swapped_first(far, near)
    ops, own, sources = call(
        fetch, [(ops.shape, F32), ((rows, 2 * tracers), BF16), (sources.shape, F32)],
        [HBM] * 3, 0, 9_000_000, [pltpu.VMEM((rows, tracers), F32), pltpu.SemaphoreType.DMA((3,))],
    )(kept(ops), kept(first_state), kept(sources))

    step_in = [HBM] * 2 + [VMEM] * 5
    step_scratch = [pltpu.SMEM(columns.shape, jnp.int32), pltpu.SMEM(live.shape, jnp.int32), window,
                    pltpu.SemaphoreType.DMA((2,))]
    first_args = (kept(columns), kept(live), ops, own, far, near, sources, last)
    first_scratch = step_scratch + [pltpu.VMEM((2 * HALO, tracers), F32), pltpu.VMEM((HALO, tracers), F32)]
    state, far, near = call(
        first_step_early, [((rows, 2 * tracers), BF16), side, side],
        step_in + [VMEM], step_flops, 6_000_000, first_scratch,
    )(*first_args)
    planes = range(0, tiles, PLANE)
    early = lax.ppermute(far, "tile", [(i, (i - 1) % tiles) for i in planes])
    state, far, near, token = call(
        first_step_late, [((rows, 2 * tracers), BF16), side, side, ((8, tracers), F32)],
        step_in + [VMEM] * 4, step_flops, 6_000_000, first_scratch, aliases={8: 0},
    )(*first_args, state, far, near)
    far = lax.ppermute(
        far, "tile",
        [(i, (i + 1 if i % 2 else i - 1) % tiles) for i in range(tiles) if i not in planes],
    )
    near = lax.ppermute(near, "tile", [(i, i ^ 1) for i in range(tiles)])
    gather, inverse, rstart = call(
        prepare, [((coarse, rows), BF16), coarse_all, coarse_all],
        [HBM, VMEM, VMEM], 4 * coarse * rows * tracers, 3_000_000,
        [pltpu.VMEM((blocks, BS), jnp.int32), pltpu.SemaphoreType.DMA((1,))],
    )(kept(cell_map.reshape(-1, BS)), own, token)
    later = lax.ppermute(rstart, "tm", [(i + 1, i) for i in range(1, slices - 1)])
    following = lax.ppermute(rstart, "tm", [(1, 0)])
    step_scratch = step_scratch + [pltpu.VMEM((rows, 2 * tracers), BF16), pltpu.VMEM((HALO, tracers), F32)]
    step_args = (kept(columns), kept(live), ops, state, far, near, sources, early, gather, inverse)
    step_flops = step_flops + 4 * coarse * rows * tracers
    fine_end, jump, far, near = call(
        second_step_first, [((rows, tracers), F32), coarse_all, coarse_rim, coarse_rim],
        step_in + [VMEM] * 4, step_flops, 8_000_000, step_scratch,
    )(*step_args, following)

    def to_slice(block, n, target):
        route = [((n - 1) * tiles + i, n * tiles + target(i) % tiles) for i in range(tiles)]
        return lax.ppermute(block, ("tm", "tile"), route)

    image = ()
    state = jump
    coarse_window = [pltpu.VMEM((reach, 2 * tracers), BF16)]
    for n in range(1, slices):
        far = to_slice(far, n, lambda i: i + 1 if i % 2 else i - 1)
        near = to_slice(near, n, lambda i: i ^ 1)
        own = to_slice(state, n, lambda i: i)
        if n == 1:
            fine_end, jump = call(
                second_step_one, [((rows, tracers), F32), coarse_all],
                step_in + [VMEM] * 4, step_flops, 8_000_000, step_scratch, aliases={10: 0},
            )(*step_args, fine_end)
            (coarse2,) = call(
                split_coarse, [((2 * coarse, reach), BF16)], [HBM, VMEM], 0, 4_000_000,
                [pltpu.VMEM((coarse, reach), F32), pltpu.SemaphoreType.DMA((1,))],
            )(kept(coarse_op), token)
        if n == 2:
            fine_end, jump, spread = call(
                second_step_others, [((rows, tracers), F32), coarse_all, ((rows, coarse), BF16)],
                step_in + [VMEM] * 4, step_flops, 8_000_000, step_scratch, aliases={10: 0},
            )(*step_args, fine_end)
        if n < slices - 1:
            state, far, near, *image = call(
                advance, [coarse_all, coarse_rim, coarse_rim, coarse_all],
                [VMEM] * (6 + len(image)), coarse_flops, 2_000_000, coarse_window,
            )(coarse2, far, own, near, jump, later, *image)
        else:
            (result,) = call(
                finish, [((rows, tracers), F32)], [VMEM] * 7,
                coarse_flops + 4 * coarse * rows * tracers, 4_000_000,
                coarse_window + [pltpu.VMEM((rows, tracers), F32), pltpu.SemaphoreType.DMA((6,))], HBM,
            )(coarse2, far, own, near, *image, spread, fine_end)
    return result[None]


def solution(mesh):
    placed = (
        P("tm", "tile", None),
        P("tile", None),
        P("tm", "tile", None, None, None),
        P("tm", "tile", None),
        P("tm", "tile"),
        P("tile", None),
        P("tile"),
    )

    return jax.shard_map(on_device, mesh=mesh, in_specs=placed, out_specs=P("tm", "tile", None), check_vma=False)
```

```python
import jax
import jax.numpy as jnp
from jax import lax
from jax.experimental import pallas as pl
from jax.experimental.pallas import tpu as pltpu
from jax.sharding import PartitionSpec as P


HALO = 256
PLANE = 16
BS = 128
F32 = jnp.float32
BF16 = jnp.bfloat16
VMEM = pl.BlockSpec(memory_space=pltpu.VMEM)
SMEM = pl.BlockSpec(memory_space=pltpu.SMEM)
HBM = pl.BlockSpec(memory_space=pltpu.HBM)


def call(kernel, outs, in_specs, flops, nbytes, scratch=(), out_spec=VMEM, aliases=None):
    return pl.pallas_call(
        kernel,
        out_shape=[jax.ShapeDtypeStruct(shape, dtype) for shape, dtype in outs],
        in_specs=in_specs,
        out_specs=[out_spec] * len(outs),
        input_output_aliases=aliases or {},
        scratch_shapes=list(scratch),
        cost_estimate=pl.CostEstimate(flops=flops, bytes_accessed=nbytes, transcendentals=0),
        compiler_params=pltpu.CompilerParams(vmem_limit_bytes=16 << 20),
    )


def kept(value):
    return pltpu.with_memory_space_constraint(value, pltpu.HBM)


def halves(value):
    high = value.astype(BF16)
    return high, (value - high.astype(F32)).astype(BF16)


def pair(value):
    return jnp.concatenate(halves(value), axis=1)


def dot(a, b):
    return jnp.dot(a, b, preferred_element_type=F32)


def folded(product):
    width = product.shape[1] // 2
    return product[:, :width] + product[:, width:]


def folded_twice(product):
    half = folded(product)
    rows = half.shape[0] // 2
    return half[:rows] + half[rows:]


def odd_tile():
    return lax.rem(lax.axis_index("tile"), 2)


def ends(starts_ref, far_ref, near_ref, sems):
    last = starts_ref.shape[0] - HALO
    odd = odd_tile()
    copies = [
        pltpu.make_async_copy(
            starts_ref.at[pl.ds(pl.multiple_of(side * last, BS), HALO), :], out_ref, sems.at[index]
        )
        for index, (side, out_ref) in enumerate(((odd, far_ref), (1 - odd, near_ref)))
    ]
    for copy in copies:
        copy.start()
    for copy in copies:
        copy.wait()


def run_copies(copies):
    for copy in copies:
        copy.start()
    return copies


def fetch(ops_ref, starts_ref, sources_ref, ops_out, own_ref, sources_out, held, sems):
    copies = run_copies([
        pltpu.make_async_copy(starts_ref, held, sems.at[0]),
        pltpu.make_async_copy(ops_ref, ops_out, sems.at[1]),
        pltpu.make_async_copy(sources_ref, sources_out, sems.at[2]),
    ])
    copies[0].wait()
    for b in range(held.shape[0] // BS):
        own_ref[b * BS:(b + 1) * BS, :] = pair(held[b * BS:(b + 1) * BS, :])
    for copy in copies[1:]:
        copy.wait()


def prepare(map_hbm, own_ref, token_ref, gather_ref, inverse_ref, rstart_ref, map_ref, sems):
    copy = pltpu.make_async_copy(map_hbm, map_ref, sems.at[0])
    copy.start()
    copy.wait()
    coarse = gather_ref.shape[0]
    cells = lax.broadcasted_iota(jnp.int32, (coarse, BS), 0)
    for b in range(map_ref.shape[0]):
        chosen = jnp.where(map_ref[b:b + 1, :] == cells, 1.0, 0.0)
        gather_ref[:, b * BS:(b + 1) * BS] = chosen.astype(BF16)
    inverse = 1.0 / dot(gather_ref[...], jnp.ones((gather_ref.shape[1], inverse_ref.shape[1]), BF16))
    inverse_ref[...] = inverse
    rstart_ref[...] = folded(dot(gather_ref[...], own_ref[...])) * inverse


def split_coarse(coarse_hbm, token_ref, coarse2_ref, coarse_ref, sems):
    copy = pltpu.make_async_copy(coarse_hbm, coarse_ref, sems.at[0])
    copy.start()
    copy.wait()
    rows = coarse_ref.shape[0]
    high, low = halves(coarse_ref[...])
    coarse2_ref[:rows, :] = high
    coarse2_ref[rows:, :] = low


def transport(cols_hbm, live_hbm, ops_ref, own_ref, far_ref, near_ref, sources_ref,
              cols_ref, live_ref, window, sems, emit):
    copies = run_copies([
        pltpu.make_async_copy(cols_hbm, cols_ref, sems.at[0]),
        pltpu.make_async_copy(live_hbm, live_ref, sems.at[1]),
    ])
    rows = own_ref.shape[0]
    blocks, slots = ops_ref.shape[:2]
    odd = odd_tile()
    window[pl.ds(pl.multiple_of(odd * (HALO + rows), BS), HALO), :] = pair(far_ref[...])
    window[pl.ds(pl.multiple_of((1 - odd) * (HALO + rows), BS), HALO), :] = pair(near_ref[...])
    window[HALO:HALO + rows, :] = own_ref[...]
    for copy in copies:
        copy.wait()
    for b in range(blocks):
        pieces, highs, lows = [], [], []
        for k in range(slots):
            at = pl.multiple_of(cols_ref[k, b] * BS, BS)
            pieces.append(window[pl.ds(at, BS), :])
            high, low = halves(jnp.where(k < live_ref[0, b], ops_ref[b, k], 0.0))
            highs.append(high)
            lows.append(low)
        pieces = jnp.concatenate(pieces, axis=0)
        operator = jnp.concatenate([jnp.concatenate(highs, axis=1), jnp.concatenate(lows, axis=1)], axis=0)
        value = folded_twice(dot(operator, pieces))
        emit(b, value + sources_ref[b * BS:(b + 1) * BS, :])


def sides(block, far_ref, near_ref, width):
    odd = odd_tile()
    last = block.shape[0] - width
    far_ref[...] = block[pl.ds(pl.multiple_of(odd * last, 64), width), :]
    near_ref[...] = block[pl.ds(pl.multiple_of((1 - odd) * last, 64), width), :]


def first_step(cols_hbm, live_hbm, ops_ref, own_ref, far_ref, near_ref, sources_ref, last_ref,
               next_ref, nfar_ref, nnear_ref, token_ref, cols_ref, live_ref, window, sems, rims, whole):
    blocks = ops_ref.shape[0]
    side = HALO // BS

    def emit(b, value):
        next_ref[b * BS:(b + 1) * BS, :] = pair(value)
        if b < side:
            rims[b * BS:(b + 1) * BS, :] = value
        if b >= blocks - side:
            at = b - blocks + 2 * side
            rims[at * BS:(at + 1) * BS, :] = value

    whole[...] = near_ref[...] + last_ref[...]
    transport(cols_hbm, live_hbm, ops_ref, own_ref, far_ref, whole, sources_ref,
              cols_ref, live_ref, window, sems, emit)
    sides(rims, nfar_ref, nnear_ref, HALO)
    token_ref[...] = jnp.zeros_like(token_ref)


def restricted_step(refs, gather_ref, inverse_ref, end_ref, jump_ref, cols_ref, live_ref, window, sems, split, whole):
    def emit(b, value):
        end_ref[b * BS:(b + 1) * BS, :] = value
        split[b * BS:(b + 1) * BS, :] = pair(value)

    whole[...] = refs[5][...] + refs[7][...]
    transport(*refs[:5], whole, refs[6], cols_ref, live_ref, window, sems, emit)
    jump_ref[...] = folded(dot(gather_ref[...], split[...])) * inverse_ref[...]


def second_step_first(*refs):
    operands, (gather_ref, inverse_ref, following_ref) = refs[:8], refs[8:11]
    end_ref, jump_ref, nfar_ref, nnear_ref = refs[11:15]

    @pl.when(lax.axis_index("tm") == 0)
    def _():
        restricted_step(operands, gather_ref, inverse_ref, end_ref, jump_ref, *refs[15:])
        jump_ref[...] = jump_ref[...] - following_ref[...]
        sides(jump_ref, nfar_ref, nnear_ref, nfar_ref.shape[0])


def second_step_rest(chosen, gather_ref, inverse_ref, operands, end_ref, jump_ref, scratch):
    @pl.when(jnp.logical_not(chosen))
    def _():
        jump_ref[...] = jnp.zeros_like(jump_ref)

    @pl.when(chosen)
    def _():
        restricted_step(operands, gather_ref, inverse_ref, end_ref, jump_ref, *scratch)


def second_step_one(*refs):
    second_step_rest(lax.axis_index("tm") == 1, refs[8], refs[9], refs[:8], refs[11], refs[12], refs[13:])


def second_step_others(*refs):
    second_step_rest(lax.axis_index("tm") > 1, refs[8], refs[9], refs[:8], refs[11], refs[12], refs[14:])
    gather_ref, spread_ref = refs[8], refs[13]
    for b in range(gather_ref.shape[1] // BS):
        spread_ref[b * BS:(b + 1) * BS, :] = gather_ref[:, b * BS:(b + 1) * BS].astype(F32).T.astype(BF16)


def fill(far_ref, own_ref, near_ref, window):
    rim, rows = far_ref.shape[0], own_ref.shape[0]
    odd = odd_tile()
    window[pl.ds(pl.multiple_of(odd * (rim + rows), 64), rim), :] = pair(far_ref[...])
    window[pl.ds(pl.multiple_of((1 - odd) * (rim + rows), 64), rim), :] = pair(near_ref[...])
    window[rim:rim + rows, :] = pair(own_ref[...])


def coarse_product(coarse2_ref, far_ref, own_ref, near_ref, window):
    fill(far_ref, own_ref, near_ref, window)
    return folded_twice(dot(coarse2_ref[...], window[...]))


def advance(coarse2_ref, far_ref, own_ref, near_ref, jump_ref, later_ref, *refs):
    state_ref, nfar_ref, nnear_ref, total_ref, window = refs[-5:]
    image = coarse_product(coarse2_ref, far_ref, own_ref, near_ref, window)
    state_ref[...] = image + (jump_ref[...] - later_ref[...])
    sides(state_ref, nfar_ref, nnear_ref, nfar_ref.shape[0])
    total_ref[...] = image if len(refs) == 5 else refs[0][...] + image


def finish(coarse2_ref, far_ref, own_ref, near_ref, image_ref, spread_ref, end_ref, out_hbm, window, held, sems):
    fill(far_ref, own_ref, near_ref, window)
    rows, tracers = own_ref.shape
    image = folded(dot(coarse2_ref[:rows, :], window[...]))
    image = image_ref[...] + image + dot(coarse2_ref[rows:, :], window[:, :tracers])
    split = pair(image)
    copies = []
    for b in range(sems.shape[0]):
        part = end_ref.shape[0] // sems.shape[0]
        rows = slice(b * part, (b + 1) * part)
        held[rows, :] = end_ref[rows, :] + folded(dot(spread_ref[rows, :], split))
        copies.append(pltpu.make_async_copy(held.at[rows, :], out_hbm.at[rows, :], sems.at[b]))
        copies[-1].start()
    for copy in copies:
        copy.wait()


def swapped(far, near):
    count = lax.axis_size("tile")
    early = [i for i in range(count) if i % PLANE < 2]
    first = lax.ppermute(near, "tile", [(i, i ^ 1) for i in early])
    far = lax.ppermute(far, "tile", [(i, (i + 1 if i % 2 else i - 1) % count) for i in range(count)])
    last = lax.ppermute(near, "tile", [(i, i ^ 1) for i in range(count) if i not in early])
    return far, first, last


def on_device(starts, sources, fine_ops, col_index, live_count, coarse_op, cell_map):
    first_state = starts[0]
    ops = fine_ops[0]
    rows, tracers = first_state.shape
    blocks, slots = ops.shape[:2]
    columns = col_index[0].T
    live = live_count
    coarse, reach = coarse_op.shape
    rim = (reach - coarse) // 2
    slices = lax.axis_size("tm")
    tiles = lax.axis_size("tile")
    window = pltpu.VMEM((rows + 2 * HALO, 2 * tracers), BF16)
    step_flops = 6 * rows * slots * BS * tracers
    coarse_flops = 6 * coarse * reach * tracers
    side = ((HALO, tracers), F32)
    coarse_rim = ((rim, tracers), F32)
    coarse_all = ((coarse, tracers), F32)

    far, near = call(ends, [side, side], [HBM], 0, 500_000, [pltpu.SemaphoreType.DMA((2,))])(kept(first_state))
    far, near, last = swapped(far, near)
    ops, own, sources = call(
        fetch, [(ops.shape, F32), ((rows, 2 * tracers), BF16), (sources.shape, F32)],
        [HBM] * 3, 0, 9_000_000, [pltpu.VMEM((rows, tracers), F32), pltpu.SemaphoreType.DMA((3,))],
    )(kept(ops), kept(first_state), kept(sources))

    step_in = [HBM] * 2 + [VMEM] * 5
    step_scratch = [pltpu.SMEM(columns.shape, jnp.int32), pltpu.SMEM(live.shape, jnp.int32), window,
                    pltpu.SemaphoreType.DMA((2,))]
    state, far, near, token = call(
        first_step, [((rows, 2 * tracers), BF16), side, side, ((8, tracers), F32)],
        step_in + [VMEM], step_flops, 6_000_000,
        step_scratch + [pltpu.VMEM((2 * HALO, tracers), F32), pltpu.VMEM((HALO, tracers), F32)],
    )(kept(columns), kept(live), ops, own, far, near, sources, last)
    far, near, last = swapped(far, near)
    gather, inverse, rstart = call(
        prepare, [((coarse, rows), BF16), coarse_all, coarse_all],
        [HBM, VMEM, VMEM], 4 * coarse * rows * tracers, 3_000_000,
        [pltpu.VMEM((blocks, BS), jnp.int32), pltpu.SemaphoreType.DMA((1,))],
    )(kept(cell_map.reshape(-1, BS)), own, token)
    later = lax.ppermute(rstart, "tm", [(i + 1, i) for i in range(1, slices - 1)])
    following = lax.ppermute(rstart, "tm", [(1, 0)])
    step_scratch = step_scratch + [pltpu.VMEM((rows, 2 * tracers), BF16), pltpu.VMEM((HALO, tracers), F32)]
    step_args = (kept(columns), kept(live), ops, state, far, near, sources, last, gather, inverse)
    step_flops = step_flops + 4 * coarse * rows * tracers
    fine_end, jump, far, near = call(
        second_step_first, [((rows, tracers), F32), coarse_all, coarse_rim, coarse_rim],
        step_in + [VMEM] * 4, step_flops, 8_000_000, step_scratch,
    )(*step_args, following)

    def to_slice(block, n, target):
        route = [((n - 1) * tiles + i, n * tiles + target(i) % tiles) for i in range(tiles)]
        return lax.ppermute(block, ("tm", "tile"), route)

    image = ()
    state = jump
    coarse_window = [pltpu.VMEM((reach, 2 * tracers), BF16)]
    for n in range(1, slices):
        far = to_slice(far, n, lambda i: i + 1 if i % 2 else i - 1)
        near = to_slice(near, n, lambda i: i ^ 1)
        own = to_slice(state, n, lambda i: i)
        if n == 1:
            fine_end, jump = call(
                second_step_one, [((rows, tracers), F32), coarse_all],
                step_in + [VMEM] * 4, step_flops, 8_000_000, step_scratch, aliases={10: 0},
            )(*step_args, fine_end)
            (coarse2,) = call(
                split_coarse, [((2 * coarse, reach), BF16)], [HBM, VMEM], 0, 4_000_000,
                [pltpu.VMEM((coarse, reach), F32), pltpu.SemaphoreType.DMA((1,))],
            )(kept(coarse_op), token)
        if n == 2:
            fine_end, jump, spread = call(
                second_step_others, [((rows, tracers), F32), coarse_all, ((rows, coarse), BF16)],
                step_in + [VMEM] * 4, step_flops, 8_000_000, step_scratch, aliases={10: 0},
            )(*step_args, fine_end)
        if n < slices - 1:
            state, far, near, *image = call(
                advance, [coarse_all, coarse_rim, coarse_rim, coarse_all],
                [VMEM] * (6 + len(image)), coarse_flops, 2_000_000, coarse_window,
            )(coarse2, far, own, near, jump, later, *image)
        else:
            (result,) = call(
                finish, [((rows, tracers), F32)], [VMEM] * 7,
                coarse_flops + 4 * coarse * rows * tracers, 4_000_000,
                coarse_window + [pltpu.VMEM((rows, tracers), F32), pltpu.SemaphoreType.DMA((6,))], HBM,
            )(coarse2, far, own, near, *image, spread, fine_end)
    return result[None]


def solution(mesh):
    placed = (
        P("tm", "tile", None),
        P("tile", None),
        P("tm", "tile", None, None, None),
        P("tm", "tile", None),
        P("tm", "tile"),
        P("tile", None),
        P("tile"),
    )

    return jax.shard_map(on_device, mesh=mesh, in_specs=placed, out_specs=P("tm", "tile", None), check_vma=False)
```
